256 devices in a mesh: row: 8 (over x, core), col: 32 (over z, y).
Axes of the slice: x: 4, y: 4, z: 8, core: 2. Of those that a mesh axis runs over, the one named last changes fastest.
Arguments:
- blocks: bfloat16 [12288, 27, 48, 48], P(('row', 'col')), may hold values from -0.59765625 to 0.59765625
- prolong: bfloat16 [12288, 48, 48], P(('row', 'col')), may hold values from -0.875 to 0.875
- columns: int32 [12288, 27], P(('row', 'col')), may hold values from 0 to 383
- aggregate: int32 [12288], P(('row', 'col')), may hold values from 0 to 15
- slots: int32 [12288, 27], P(('row', 'col')), may hold values from 0 to 26
Outputs:
- coarse: float32 [128, 27, 2304], P('row', None, 'col')
The draws below stay inside these ranges and needn't reach their ends.
Inputs may be any that keep to these rules, and one draw needn't show every extreme that they name: `columns`: a fine block row's neighbours all lie in its column tile: the fine block rows of the devices with the same col index, in order of their row index.
All inputs are finite; a program needn't handle non-finite values.
Results may differ from the reference program's by a relative error of at most 0.0029.
Values may be sent and summed in bfloat16 or wider, within the bound.
No kernel may reach another device: no remote copies, remote signals or barrier semaphores. Data moves between devices by JAX's collectives and lax.ppermute only.
A program may use at most 192 MiB of HBM per device.

```python
import jax
import jax.numpy as jnp
from jax import lax

B = 48
K = 27
KC = 27
ROWS_DEV = 48
CR_SLAB = 16
NB = 12288
N_ROW = 8
N_COL = 32


def set_ends(result, key, least, high):
    extent = result.shape
    index_at = [jax.random.randint(jax.random.fold_in(key, axis), (), 0, extent[axis]) for axis in range(len(extent))]
    result = result.at[tuple(index_at)].set(least)
    longest = extent.index(max(extent))
    index_at[longest] = (index_at[longest] + 1) % extent[longest]
    return result.at[tuple(index_at)].set(high)


def levels(own_key, dims, shards, low, largest):
    gain = 1.0
    for axis_at, blocks in shards:
        steps = jax.random.uniform(jax.random.fold_in(jax.random.fold_in(own_key, 6), axis_at), (blocks,), jnp.float32, low / len(shards), largest / len(shards))
        gain = gain * jnp.repeat(jnp.exp(steps), dims[axis_at] // blocks).reshape((-1,) + (1,) * (len(dims) - 1 - axis_at))
    return gain


def normal_values(rng, dims, scale, most, shards=(), kind=jnp.bfloat16):
    level = levels(rng, dims, shards, -0.22, 0.18) if shards else 1.0
    result = jax.random.normal(rng, dims, jnp.float32) * scale * level
    return jnp.minimum(jnp.maximum(result, -most), most).astype(kind)


def setup_inputs(seed: int = 0) -> dict:
    keys = jax.random.split(jax.random.key(seed), 6)
    return {
        "blocks": normal_values(keys[0], (NB, K, B, B), 0.1, 0.59765625, ((0, 256),)),
        "prolong": normal_values(keys[1], (NB, B, B), B ** -0.5, 0.875, ((0, 256),)),
        "columns": set_ends(jax.random.randint(keys[2], (NB, K), 0, ROWS_DEV * N_ROW), jax.random.fold_in(keys[2], 1), 0, (ROWS_DEV * N_ROW) - 1).astype(jnp.int32),
        "aggregate": set_ends(jax.random.randint(keys[3], (NB,), 0, CR_SLAB), jax.random.fold_in(keys[3], 1), 0, CR_SLAB - 1).astype(jnp.int32),
        "slots": set_ends(jax.random.randint(keys[4], (NB, K), 0, KC), jax.random.fold_in(keys[4], 1), 0, KC - 1).astype(jnp.int32),
    }


def reference(blocks, prolong, columns, aggregate, slots):
    owners_all = N_ROW * N_COL
    block_parts = blocks.reshape(owners_all, ROWS_DEV, K, B, B)
    prolong_parts = prolong.reshape(owners_all, ROWS_DEV, B, B)
    column_parts = columns.reshape(owners_all, ROWS_DEV, K)
    aggregate_parts = aggregate.reshape(owners_all, ROWS_DEV)
    slot_parts = slots.reshape(owners_all, ROWS_DEV, K)

    def accumulate(total, item):
        owner, local_blocks, local_prolong, local_columns, local_aggregate, local_slots = item
        slab_index = owner // N_COL
        tile_index = owner % N_COL
        neighbour = (local_columns // ROWS_DEV) * (N_COL * ROWS_DEV) + tile_index * ROWS_DEV + local_columns % ROWS_DEV
        picked = jnp.take(prolong, neighbour.astype(jnp.int32), axis=0)
        product = jnp.einsum("rkab,rkbc->rkac", local_blocks.astype(jnp.float32), picked.astype(jnp.float32))
        product = lax.optimization_barrier(product.astype(jnp.bfloat16)).astype(jnp.float32)
        term = jnp.einsum("rba,rkbc->rkac", local_prolong.astype(jnp.float32), product)
        target = ((slab_index * CR_SLAB + local_aggregate)[:, None] * KC + local_slots).astype(jnp.int32)
        total = total.at[target.reshape(-1)].add(term.reshape(-1, B * B))
        return total, None

    owners = jnp.arange(owners_all, dtype=jnp.int32)
    start = jnp.zeros((N_ROW * CR_SLAB * KC, B * B), jnp.float32)
    total, _ = lax.scan(accumulate, start, (owners, block_parts, prolong_parts, column_parts, aggregate_parts, slot_parts))
    return total.reshape(N_ROW * CR_SLAB, KC, B * B)
```

```python
import functools
import jax, jax.numpy as jnp
from jax import lax
from jax.experimental import pallas as pl
from jax.experimental.pallas import tpu as pltpu
bf, f32 = jnp.bfloat16, jnp.float32
B, K, KC, CR, R = 48, 27, 27, 16, 48
T = KC * CR
H = B // 2
HALF = T * H
PAIRS = (K + 1) // 2
PLACES = [[(0, 0), (0, 1), (1, 0)], [(0, 2), (1, 1), (1, 2)], [(0, 3), (0, 4), (1, 3)], [(0, 5), (1, 4), (1, 5)]]

def pack_kernel(p_ref, o_ref):
    for g in range(R // 8):
        o_ref[g * B:(g + 1) * B, :] = jnp.concatenate(
            [p_ref[8 * g + m].astype(f32).T for m in range(8)], axis=1).astype(bf)

def pack(p):
    return pl.pallas_call(pack_kernel, out_shape=jax.ShapeDtypeStruct((R // 8 * B, 8 * B), bf))(p)

def main_kernel(G, cols, slots, agg, blk_hbm, pro, pg, out, blk, plo, phi, alo, ahi, bufa, bufb, ta, tb, sems):
    CH = 4
    def copy(n):
        return pltpu.make_async_copy(blk_hbm.at[pl.ds(n * CH, CH)], blk.at[pl.ds(n * CH, CH)], sems.at[n])
    for n in range(R // CH):
        copy(n).start()
    if True:
        for m in range(8):
            first = (48 * m // 128) * 128
            wide = min(256, 384 - first)
            row = lax.broadcasted_iota(jnp.int32, (wide, 256), 0) + first - 48 * m
            lane = lax.broadcasted_iota(jnp.int32, (wide, 256), 1)
            inside = (row >= 0) & (row < 48)
            pick = (inside & ((lane == row) | (lane == row + 128 + 48))).astype(f32).astype(bf)
            def unpack(n, c):
                x = pg[pl.ds(pl.multiple_of(n * 192, 192), 192), first:first + wide]
                y = jnp.dot(x, pick, preferred_element_type=f32).astype(bf)
                at = pl.multiple_of(m * 48 * B + n * 192, 192)
                plo[pl.ds(at, 192), :] = y[:, :128]
                phi[pl.ds(at, 192), :] = y[:, 128:]
                z = pl.multiple_of((m * 12 + n) * 216, 8)
                alo[pl.ds(z, 216), :] = jnp.zeros((216, 128), f32)
                ahi[pl.ds(z, 216), :] = jnp.zeros((216, 128), f32)
                return c
            lax.fori_loop(0, 12, unpack, 0)

    bufa[:, 96:] = jnp.zeros((PAIRS * B, 32), bf)
    bufb[:, 96:] = jnp.zeros((PAIRS * B, 32), bf)

    def phase1(i, n, buf):
        two = range(2 * n, min(2 * n + 2, K))
        at = []
        for k in two:
            j = cols[k, i]
            at.append(pl.multiple_of(((j & 7) * 48 + (j >> 3)) * B, B))
        lhs = plo[pl.ds(at[0], B), :]
        zero = jnp.zeros((B, B), bf)
        if len(two) == 2:
            lhs = lhs + phi[pl.ds(at[1], B), :]
            w = jnp.concatenate([jnp.concatenate([blk[i, two[0]], zero], axis=1),
                                 jnp.concatenate([zero, blk[i, two[1]]], axis=1)], axis=0)
            p = lax.dot_general(lhs[:, :96], w, (((1,), (1,)), ((), ())), preferred_element_type=f32)
        else:
            w = jnp.concatenate([jnp.concatenate([blk[i, two[0]], zero], axis=1), jnp.zeros((B, 2 * B), bf)], axis=0)
            p = lax.dot_general(lhs[:, :96], w, (((1,), (1,)), ((), ())), preferred_element_type=f32)
        buf[n * B:(n + 1) * B, :96] = p.astype(bf)

    def phase2(w, n, buf, tbuf):
        tbuf[n * B:(n + G) * B, :] = jnp.dot(buf[n * B:(n + G) * B, :], w, preferred_element_type=f32)

    def add(i, base, n, tbuf):
        for k in range(2 * n, min(2 * n + 2, K)):
            at = pl.multiple_of((slots[k, i] * CR + base) * H, 8)
            acc = ahi if k & 1 else alo
            for h in range(2):
                acc[pl.ds(at + h * HALF, H), :] += tbuf[n * B + h * H:n * B + (h + 1) * H, :]

    def both(i1, buf1, i2, buf2, tbuf):
        w = pro[i2]
        base = agg[i2]
        for n in range(PAIRS):
            if n % G == 0:
                phase2(w, n, buf2, tbuf)
            if True:
                phase1(i1, n, buf1)
            if True:
                add(i2, base, n, tbuf)

    if True:
        copy(0).wait()
        for n in range(PAIRS):
            phase1(0, n, bufa)

        def rows(q, c):
            both(2 * q + 1, bufb, 2 * q, bufa, ta)
            @pl.when((q & 1 == 1) & (q < 23))
            def _():
                copy((q + 1) // 2).wait()
            both(jnp.minimum(2 * q + 2, R - 1), bufa, 2 * q + 1, bufb, tb)
            return c
        lax.fori_loop(0, R // 2, rows, 0)
    else:
        for n in range(R // CH):
            copy(n).wait()

    if True:
        def flush(n, c):
            low = lax.broadcasted_iota(jnp.int32, (128, 128), 1) < B
            halves = []
            for h in range(2):
                at = pl.multiple_of(h * HALF + n * 128, 128)
                x = jnp.where(low, alo[pl.ds(at, 128), :], ahi[pl.ds(at, 128), :]).T
                halves.append(x[:B] + x[B:2 * B])
            at = pl.multiple_of(n * 128, 128)
            for y in range(4):
                rows = [halves[h][8 * u:8 * u + 8] for h, u in PLACES[y]]
                out[y, :, pl.ds(at, 128)] = jnp.concatenate(rows, axis=0).astype(bf)
            return c
        lax.fori_loop(0, HALF // 128, flush, 0)

def main(colsT, slotsT, agg, blocks, wide, pg, G=14):
    return pl.pallas_call(
        functools.partial(main_kernel, G),
        out_shape=jax.ShapeDtypeStruct((4, 24, HALF), bf),
        in_specs=[pl.BlockSpec(memory_space=pltpu.SMEM)] * 3 + [pl.BlockSpec(memory_space=pl.ANY)] + [pl.BlockSpec(memory_space=pltpu.VMEM)] * 2,
        out_specs=pl.BlockSpec(memory_space=pltpu.VMEM),
        scratch_shapes=[pltpu.VMEM((R, K, B, B), bf)] + [pltpu.VMEM((384 * B, 128), bf)] * 2 + [pltpu.VMEM((2 * HALF, 128), f32)] * 2
            + [pltpu.VMEM((PAIRS * B, 128), bf)] * 2 + [pltpu.VMEM((PAIRS * B, 128), f32)] * 2 + [pltpu.SemaphoreType.DMA((12,))],
        compiler_params=pltpu.CompilerParams(vmem_limit_bytes=63 << 20),
    )(colsT, slotsT, agg, blocks, wide, pg)

def weights_kernel(p_ref, o_ref):
    a = lax.broadcasted_iota(jnp.int32, (B, 128), 0)
    lane = lax.broadcasted_iota(jnp.int32, (B, 128), 1)
    place = (a % 6) * 8 + a // 6
    first = (lane == place).astype(f32).astype(bf)
    second = (lane == place + B).astype(f32).astype(bf)
    o_ref[:, 2 * B:, :] = jnp.zeros((R, 128 - 2 * B, 128), bf)
    def body(i, c):
        p = p_ref[i]
        o_ref[i, :B, :] = jnp.dot(p, first, preferred_element_type=f32).astype(bf)
        o_ref[i, B:2 * B, :] = jnp.dot(p, second, preferred_element_type=f32).astype(bf)
        return c
    lax.fori_loop(0, R, body, 0, unroll=4)

def weights(p):
    return pl.pallas_call(weights_kernel, out_shape=jax.ShapeDtypeStruct((R, 128, 128), bf))(p)

BLK = HALF // 128

def sum_kernel(x_ref, o_ref, buf):
    def body(b, c):
        at = pl.multiple_of(b * 128, 128)
        s = x_ref[0, :, pl.ds(at, 128)].astype(f32)
        for y in range(1, 4):
            s = s + x_ref[y, :, pl.ds(at, 128)].astype(f32)
        for g in range(3):
            buf[pl.ds(g * BLK + b, 8, stride=256), :] = s[8 * g:8 * g + 8]
        return c
    lax.fori_loop(0, BLK, body, 0, unroll=3)
    for z in range(8):
        o_ref[z] = buf[z * 256:(z + 1) * 256, :].astype(bf)

def sum_y(x):
    return pl.pallas_call(sum_kernel, out_shape=jax.ShapeDtypeStruct((8, 256, 128), bf),
                          scratch_shapes=[pltpu.VMEM((8 * 256, 128), f32)])(x)

def final_kernel(par_ref, x_ref, o_ref, tot):
    tot[...] = functools.reduce(lambda p, q: p + q, [x_ref[z].astype(f32) for z in range(8)])
    odd = par_ref[0]
    acc = jnp.zeros((T, 128), f32)
    lane = lax.broadcasted_iota(jnp.int32, (KC, CR, 128), 2)
    agg = lax.broadcasted_iota(jnp.int32, (KC, CR, 128), 1)
    l0 = lax.broadcasted_iota(jnp.int32, (128, 128), 0)
    l1 = lax.broadcasted_iota(jnp.int32, (128, 128), 1)
    for w in range(3):
        mask = (lane + w * 128) // H == agg
        for g in range(3):
            place = jnp.where(odd == 1, (1, 0, 2)[g], (0, 2, 1)[g])
            pick = ((l0 + w * 128) % H + place * H == l1).astype(f32).astype(bf)
            x = tot[pl.ds(g * BLK + w, KC, stride=3), :]
            for _ in range(3):
                top = x.astype(bf).astype(f32)
                x = x - top
                wide = jnp.where(mask, jnp.broadcast_to(top[:, None, :], (KC, CR, 128)), 0.0).reshape(T, 128).astype(bf)
                acc = acc + jnp.dot(wide, pick, preferred_element_type=f32)
    o_ref[...] = acc[:, :72].reshape(KC, CR, 72)

def final(par, x):
    return pl.pallas_call(final_kernel, out_shape=jax.ShapeDtypeStruct((KC, CR, 72), f32),
                          in_specs=[pl.BlockSpec(memory_space=pltpu.SMEM), pl.BlockSpec(memory_space=pltpu.VMEM)],
                          scratch_shapes=[pltpu.VMEM((256, 128), f32)])(par, x)

YG = [[z * 4 + y for y in range(4)] for z in range(8)]
ZG = [[z * 4 + y for z in range(8)] for y in range(4)]

def shards(blocks, prolong, columns, aggregate, slots):
    packed = pack(prolong)
    tile = lax.all_gather(packed, "row", axis=0, tiled=True)
    part = main(columns.T, slots.T, aggregate, blocks, weights(prolong), tile)
    part = lax.all_to_all(part, "col", 0, 0, axis_index_groups=YG, tiled=True)
    part = sum_y(part)
    part = lax.all_to_all(part, "col", 0, 0, axis_index_groups=ZG, tiled=True)
    odd = lax.axis_index("col") & 1
    return final(odd.reshape(1), part).transpose(1, 0, 2)


def solution(mesh):
    return jax.shard_map(
        shards,
        mesh=mesh,
        in_specs=(
            jax.sharding.PartitionSpec(("row", "col"), None, None, None),
            jax.sharding.PartitionSpec(("row", "col"), None, None),
            jax.sharding.PartitionSpec(("row", "col"), None),
            jax.sharding.PartitionSpec(("row", "col")),
            jax.sharding.PartitionSpec(("row", "col"), None),
        ),
        out_specs=jax.sharding.PartitionSpec("row", None, "col"),
        check_vma=False,
    )
```

```python
import functools
import jax, jax.numpy as jnp
from jax import lax
from jax.experimental import pallas as pl
from jax.experimental.pallas import tpu as pltpu
bf, f32 = jnp.bfloat16, jnp.float32
B, K, KC, CR, R = 48, 27, 27, 16, 48
T = KC * CR
H = B // 2
HALF = T * H
PAIRS = (K + 1) // 2
PIECE = R // 2 * B
PLACES = [[(0, 0), (0, 1), (1, 0)], [(0, 2), (1, 1), (1, 2)], [(0, 3), (0, 4), (1, 3)], [(0, 5), (1, 4), (1, 5)]]

def pack_kernel(p_ref, o_ref):
    pad = jnp.zeros((B, 128 - 2 * B), f32)
    for n in range(R // 2):
        two = [p_ref[2 * n + m].astype(f32).T for m in range(2)]
        o_ref[n * B:(n + 1) * B, :] = jnp.concatenate(two + [pad], axis=1).astype(bf)

def pack(p):
    return pl.pallas_call(pack_kernel, out_shape=jax.ShapeDtypeStruct((PIECE, 128), bf))(p)

def main_kernel(G, opt, cols, slots, agg, blk_hbm, pro_hbm, *rest):
    pieces, (out, blk, pro, tile, alo, ahi, bufa, bufb, ta, tb, sems, psems) = rest[:-12], rest[-12:]
    CH = 4
    def copy(n):
        return pltpu.make_async_copy(blk_hbm.at[pl.ds(n * CH, CH)], blk.at[pl.ds(n * CH, CH)], sems.at[n])
    first = []
    rows0 = 0
    for n, piece in enumerate(pieces):
        size = piece.shape[0]
        first.append(pltpu.make_async_copy(piece, tile.at[pl.ds(rows0, size)], psems.at[n]))
        rows0 += size
    first.append(pltpu.make_async_copy(pro_hbm, pro, psems.at[len(pieces)]))
    for c in first:
        c.start()
    for n in range(R // CH):
        copy(n).start()

    def zero(n, c):
        z = pl.multiple_of(n * 648, 8)
        alo[pl.ds(z, 648), :] = jnp.zeros((648, 128), f32)
        ahi[pl.ds(z, 648), :] = jnp.zeros((648, 128), f32)
        return c
    if 'noinit' not in opt:
        lax.fori_loop(0, 32, zero, 0)

    bufa[...] = jnp.zeros((PAIRS * B, 128), bf)
    bufb[...] = jnp.zeros((PAIRS * B, 128), bf)

    lane = lax.broadcasted_iota(jnp.int32, (B, 128), 1)

    def phase1(i, n, buf):
        lhs, rhs = [], []
        for k in range(2 * n, min(2 * n + 2, K)):
            j = cols[k, i]
            lhs.append(tile[pl.ds(pl.multiple_of((j >> 1) * B, B), B), :])
            a = blk[i, k]
            a = jnp.concatenate([a, a, jnp.zeros((B, 128 - 2 * B), bf)], axis=1)
            odd = j & 1
            rhs.append(jnp.where((lane >= B * odd) & (lane < B * odd + B), a, jnp.zeros((B, 128), bf)))
        if len(lhs) == 2:
            zero = jnp.zeros((B, 128), bf)
            w = jnp.concatenate([jnp.concatenate([rhs[0], zero], axis=1), jnp.concatenate([zero, rhs[1]], axis=1)], axis=0)
            p = lax.dot_general(jnp.concatenate(lhs, axis=1), w, (((1,), (1,)), ((), ())), preferred_element_type=f32)
            buf[n * B:(n + 1) * B, :96] = p.astype(bf)
        else:
            p = lax.dot_general(lhs[0], rhs[0], (((1,), (1,)), ((), ())), preferred_element_type=f32)
            buf[n * B:(n + 1) * B, :48] = p.astype(bf)

    def phase2(w, n, buf, tbuf):
        tbuf[n * B:(n + G) * B, :] = jnp.dot(buf[n * B:(n + G) * B, :], w, preferred_element_type=f32)

    def add(i, base, n, tbuf):
        for k in range(2 * n, min(2 * n + 2, K)):
            at = pl.multiple_of((slots[k, i] * CR + base) * H, 8)
            acc = ahi if k & 1 else alo
            for h in range(2):
                acc[pl.ds(at + h * HALF, H), :] += tbuf[n * B + h * H:n * B + (h + 1) * H, :]

    def both(i1, buf1, i2, buf2, tbuf):
        w = pro[i2]
        base = agg[i2]
        for n in range(PAIRS):
            if 'nop2' not in opt and n % G == 0:
                phase2(w, n, buf2, tbuf)
            if 'nop1' not in opt:
                phase1(i1, n, buf1)
            if 'noacc' not in opt:
                add(i2, base, n, tbuf)

    if True:
        for c in first:
            c.wait()
        copy(0).wait()
        for n in range(PAIRS):
            phase1(0, n, bufa)

        def rows(q, c):
            both(2 * q + 1, bufb, 2 * q, bufa, ta)
            @pl.when((q & 1 == 1) & (q < 23))
            def _():
                copy((q + 1) // 2).wait()
            both(jnp.minimum(2 * q + 2, R - 1), bufa, 2 * q + 1, bufb, tb)
            return c
        if 'norows' not in opt:
            lax.fori_loop(0, R // 2, rows, 0)
    else:
        for n in range(R // CH):
            copy(n).wait()

    if True:
        def flush(n, c):
            low = lax.broadcasted_iota(jnp.int32, (128, 128), 1) < B
            halves = []
            for h in range(2):
                at = pl.multiple_of(h * HALF + n * 128, 128)
                x = jnp.where(low, alo[pl.ds(at, 128), :], ahi[pl.ds(at, 128), :]).T
                halves.append(x[:B] + x[B:2 * B])
            at = pl.multiple_of(n * 128, 128)
            for y in range(4):
                rows = [halves[h][8 * u:8 * u + 8] for h, u in PLACES[y]]
                out[y, :, pl.ds(at, 128)] = jnp.concatenate(rows, axis=0).astype(bf)
            return c
        lax.fori_loop(0, HALF // 128 if 'noflush' not in opt else 1, flush, 0)

def main(colsT, slotsT, agg, blocks, wide, pieces, G=14, opt=()):
    hbm = pl.BlockSpec(memory_space=pl.ANY)
    return pl.pallas_call(
        functools.partial(main_kernel, G, opt),
        out_shape=jax.ShapeDtypeStruct((4, 24, HALF), bf),
        in_specs=[pl.BlockSpec(memory_space=pltpu.SMEM)] * 3 + [hbm] * (2 + len(pieces)),
        out_specs=pl.BlockSpec(memory_space=pltpu.VMEM),
        scratch_shapes=[pltpu.VMEM((R, K, B, B), bf), pltpu.VMEM((R, 128, 128), bf), pltpu.VMEM((8 * PIECE, 128), bf)]
            + [pltpu.VMEM((2 * HALF, 128), f32)] * 2 + [pltpu.VMEM((PAIRS * B, 128), bf)] * 2
            + [pltpu.VMEM((PAIRS * B, 128), f32)] * 2 + [pltpu.SemaphoreType.DMA((12,)), pltpu.SemaphoreType.DMA((len(pieces) + 1,))],
        compiler_params=pltpu.CompilerParams(vmem_limit_bytes=63 << 20),
    )(colsT, slotsT, agg, blocks, wide, *pieces)

def weights_kernel(p_ref, o_ref):
    a = lax.broadcasted_iota(jnp.int32, (B, 128), 0)
    lane = lax.broadcasted_iota(jnp.int32, (B, 128), 1)
    place = (a % 6) * 8 + a // 6
    first = (lane == place).astype(f32).astype(bf)
    second = (lane == place + B).astype(f32).astype(bf)
    o_ref[:, 2 * B:, :] = jnp.zeros((R, 128 - 2 * B, 128), bf)
    def body(i, c):
        p = p_ref[i]
        o_ref[i, :B, :] = jnp.dot(p, first, preferred_element_type=f32).astype(bf)
        o_ref[i, B:2 * B, :] = jnp.dot(p, second, preferred_element_type=f32).astype(bf)
        return c
    lax.fori_loop(0, R, body, 0, unroll=4)

def weights(p):
    return pl.pallas_call(weights_kernel, out_shape=jax.ShapeDtypeStruct((R, 128, 128), bf))(p)

BLK = HALF // 128

def sum_kernel(x_ref, o_ref, buf):
    def body(b, c):
        at = pl.multiple_of(b * 128, 128)
        s = x_ref[0, :, pl.ds(at, 128)].astype(f32)
        for y in range(1, 4):
            s = s + x_ref[y, :, pl.ds(at, 128)].astype(f32)
        for g in range(3):
            buf[pl.ds(g * BLK + b, 8, stride=256), :] = s[8 * g:8 * g + 8]
        return c
    lax.fori_loop(0, BLK, body, 0, unroll=3)
    for z in range(8):
        o_ref[z] = buf[z * 256:(z + 1) * 256, :].astype(bf)

def sum_y(x):
    return pl.pallas_call(sum_kernel, out_shape=jax.ShapeDtypeStruct((8, 256, 128), bf),
                          scratch_shapes=[pltpu.VMEM((8 * 256, 128), f32)])(x)

def final_kernel(par_ref, x_ref, o_ref, tot):
    tot[...] = functools.reduce(lambda p, q: p + q, [x_ref[z].astype(f32) for z in range(8)])
    odd = par_ref[0]
    acc = jnp.zeros((T, 128), f32)
    lane = lax.broadcasted_iota(jnp.int32, (KC, CR, 128), 2)
    agg = lax.broadcasted_iota(jnp.int32, (KC, CR, 128), 1)
    l0 = lax.broadcasted_iota(jnp.int32, (128, 128), 0)
    l1 = lax.broadcasted_iota(jnp.int32, (128, 128), 1)
    for w in range(3):
        mask = (lane + w * 128) // H == agg
        for g in range(3):
            place = jnp.where(odd == 1, (1, 0, 2)[g], (0, 2, 1)[g])
            pick = ((l0 + w * 128) % H + place * H == l1).astype(f32).astype(bf)
            x = tot[pl.ds(g * BLK + w, KC, stride=3), :]
            for _ in range(3):
                top = x.astype(bf).astype(f32)
                x = x - top
                wide = jnp.where(mask, jnp.broadcast_to(top[:, None, :], (KC, CR, 128)), 0.0).reshape(T, 128).astype(bf)
                acc = acc + jnp.dot(wide, pick, preferred_element_type=f32)
    o_ref[...] = acc[:, :72].reshape(KC, CR, 72)

def final(par, x):
    return pl.pallas_call(final_kernel, out_shape=jax.ShapeDtypeStruct((KC, CR, 72), f32),
                          in_specs=[pl.BlockSpec(memory_space=pltpu.SMEM), pl.BlockSpec(memory_space=pltpu.VMEM)],
                          scratch_shapes=[pltpu.VMEM((256, 128), f32)])(par, x)

YG = [[z * 4 + y for y in range(4)] for z in range(8)]
ZG = [[z * 4 + y for z in range(8)] for y in range(4)]

def gather(p):
    def along(x, by):
        return lax.ppermute(x, "row", [(i, (i + 2 * by) % 8) for i in range(8)])
    def across(x):
        return lax.ppermute(x, "row", [(i, i ^ 1) for i in range(8)])
    half = PIECE // 2
    left, right = along(p, 1), along(p, -1)
    far = [along(left[:half], 1), along(right[half:], -1)]
    mine = [p, right, left] + far
    return mine + [across(q) for q in mine]

def places(columns):
    row = lax.axis_index("row")
    owner = columns // R
    apart = (owner // 2 - row // 2) & 3
    at = jnp.where(apart == 3, 2, jnp.where(apart == 2, 3, apart)) + 4 * ((owner ^ row) & 1)
    return at * R + columns % R

def shards(blocks, prolong, columns, aggregate, slots):
    pieces = gather(pack(prolong))
    part = main(places(columns).T, slots.T, aggregate, blocks, weights(prolong), pieces)
    part = lax.all_to_all(part, "col", 0, 0, axis_index_groups=YG, tiled=True)
    part = sum_y(part)
    part = lax.all_to_all(part, "col", 0, 0, axis_index_groups=ZG, tiled=True)
    odd = lax.axis_index("col") & 1
    return final(odd.reshape(1), part).transpose(1, 0, 2)


def solution(mesh):
    return jax.shard_map(
        shards,
        mesh=mesh,
        in_specs=(
            jax.sharding.PartitionSpec(("row", "col"), None, None, None),
            jax.sharding.PartitionSpec(("row", "col"), None, None),
            jax.sharding.PartitionSpec(("row", "col"), None),
            jax.sharding.PartitionSpec(("row", "col")),
            jax.sharding.PartitionSpec(("row", "col"), None),
        ),
        out_specs=jax.sharding.PartitionSpec("row", None, "col"),
        check_vma=False,
    )
```

```python
import functools
import jax, jax.numpy as jnp
from jax import lax
from jax.experimental import pallas as pl
from jax.experimental.pallas import tpu as pltpu
bf, f32 = jnp.bfloat16, jnp.float32
B, K, KC, CR, R = 48, 27, 27, 16, 48
PAIRS = (K + 1) // 2
PIECE = R // 2 * B
HALF = B // 2
TILE = 8 * PIECE
FULL = (0, 2, 3, 5)
SPLIT = ((1, 0), (1, 1), (4, 0), (4, 1))

def slots_of(chunks):
    rows = CR // chunks
    return rows, -(-KC * rows // 16) * 16 // rows

def pack_kernel(p_ref, o_ref):
    pad = jnp.zeros((B, 128 - 2 * B), bf)
    for n in range(R // 2):
        o_ref[n * B:(n + 1) * B, :] = jnp.concatenate([p_ref[2 * n], p_ref[2 * n + 1], pad], axis=1)

def pack(p):
    return pl.pallas_call(pack_kernel, out_shape=jax.ShapeDtypeStruct((PIECE, 128), bf))(p)

def turn_kernel(p_ref, o_ref):
    row = lax.broadcasted_iota(jnp.int32, (B, B), 0)
    a = lax.broadcasted_iota(jnp.int32, (B, B), 1)
    pick = (row == (a % 6) * 8 + a // 6).astype(f32).astype(bf)
    for i in range(R):
        o_ref[i] = lax.dot_general(pick, p_ref[i], (((1,), (1,)), ((), ())), preferred_element_type=f32).astype(bf)

def turn(p):
    return pl.pallas_call(turn_kernel, out_shape=jax.ShapeDtypeStruct((R, B, B), bf),
                          cost_estimate=pl.CostEstimate(flops=10**7, bytes_accessed=2 * 10**6, transcendentals=0))(p)

def place_kernel_matrix(n, step, off):
    row = lax.broadcasted_iota(jnp.int32, (n * 128, 384), 0)
    col = lax.broadcasted_iota(jnp.int32, (n * 128, 384), 1)
    t, c = col // step, col % step
    return (row == (t // 2) * 128 + (t % 2) * B + off + c).astype(f32).astype(bf)

def main_kernel(q, chunks, cols, slots, agg, here, blk_hbm, turned_hbm, *rest):
    keeps = q == 0 and chunks > 1
    outs = 5 if keeps else 4
    npieces = len(rest) - 15 - outs
    pieces, (*sends, ), (out, osems, blk, turned, tile, lo, hi, bufa, bufb, only, full_ref, half_ref, todo, sems, psems) = (
        rest[:npieces], rest[npieces:npieces + outs], rest[npieces + outs:])
    crows, kslots = slots_of(chunks)
    total = crows * kslots
    first = []
    at = 0
    for n, piece in enumerate(pieces):
        first.append(pltpu.make_async_copy(piece, tile.at[pl.ds(at, piece.shape[0])], psems.at[n]))
        at += piece.shape[0]
    first.append(pltpu.make_async_copy(turned_hbm, turned, psems.at[npieces]))
    for c in first:
        c.start()

    def copy(r):
        return pltpu.make_async_copy(blk_hbm.at[todo[r]], blk.at[r], sems.at[r])
    todo[0] = 0
    def collect(i, n):
        ours = (agg[i] // crows == q)
        @pl.when(ours)
        def _():
            todo[n] = i
            copy(n).start()
        return n + ours.astype(jnp.int32)
    count = lax.fori_loop(0, R, collect, 0)

    def zero(n, c):
        z = pl.multiple_of(n * B * 4, 8)
        lo[pl.ds(z, B * 4), :] = jnp.zeros((B * 4, 128), f32)
        hi[pl.ds(z, B * 4), :] = jnp.zeros((B * 4, 128), f32)
        return c
    lax.fori_loop(0, total // 8, zero, 0)
    lane = lax.broadcasted_iota(jnp.int32, (32, 128), 1)
    row = lax.broadcasted_iota(jnp.int32, (32, 128), 0)
    only[...] = ((lane >= B * (row // 16)) & (lane < B * (row // 16) + B)).astype(f32).astype(bf)
    full_ref[...] = place_kernel_matrix(4, B, 0)
    for h in range(2):
        half_ref[h] = place_kernel_matrix(8, HALF, h * HALF)
    for c in first:
        c.wait()

    if q == 0:
        l0 = lax.broadcasted_iota(jnp.int32, (128, 128), 0)
        l1 = lax.broadcasted_iota(jnp.int32, (128, 128), 1)
        change = ((l0 < 2 * B) & (l1 == jnp.where(l0 < B, l0 + B, l0 - B))).astype(f32).astype(bf)
        def swap(n, c):
            z = pl.multiple_of(n * 1152, 1152)
            tile[pl.ds(TILE + z, 1152), :] = jnp.dot(tile[pl.ds(z, 1152), :], change, preferred_element_type=f32).astype(bf)
            return c
        lax.fori_loop(0, TILE // 1152, swap, 0)
        if keeps:
            keep = pltpu.make_async_copy(tile.at[pl.ds(TILE, TILE)], sends[4], psems.at[0])
            keep.start()

    def target(k, i, row):
        return slots[k, i] * crows + row

    def phase1(r, i, n, buf):
        row = agg[i] - q * crows
        ks = list(range(2 * n, min(2 * n + 2, K)))
        w = []
        for k in ks:
            j = cols[k, i]
            odd = target(k, i, row) & 1
            at = pl.multiple_of((j >> 1) * B + ((j & 1) ^ odd) * TILE, B)
            mask = only[pl.ds(pl.multiple_of(odd * 16, 16), 16), :]
            w.append(tile[pl.ds(at, B), :] * jnp.concatenate([mask] * 3, axis=0))
        if len(ks) == 2:
            none = jnp.zeros((B, 128), bf)
            lhs = jnp.concatenate([blk[r, ks[0]], blk[r, ks[1]]], axis=1)
            p = jnp.dot(lhs, jnp.concatenate([jnp.concatenate([w[0], none], axis=1), jnp.concatenate([none, w[1]], axis=1)], axis=0), preferred_element_type=f32)
            buf[:, n * 256:(n + 1) * 256] = p.astype(bf)
        else:
            for m, k in enumerate(ks):
                buf[:, k * 128:(k + 1) * 128] = jnp.dot(blk[r, k], w[m], preferred_element_type=f32).astype(bf)

    def phase2(i, real, row, n, buf):
        term = jnp.dot(turned[i], buf[:, n * 256:(n + 1) * 256], preferred_element_type=f32)
        for m in range(2):
            k = 2 * n + m
            if k < K:
                t = jnp.where(real, target(k, i, row) >> 1, total // 2)
                acc = hi if m & 1 else lo
                acc[pl.ds(pl.multiple_of(t * B, B), B), :] += term[:, m * 128:(m + 1) * 128]

    def both(r1, buf1, r2, buf2):
        r1 = jnp.minimum(r1, count - 1)
        i1, i2 = todo[r1], todo[jnp.minimum(r2, count - 1)]
        real = r2 < count
        row = agg[i2] - q * crows
        for n in range(PAIRS):
            phase2(i2, real, row, n, buf2)
            phase1(r1, i1, n, buf1)

    def arrived(r):
        @pl.when(r < count)
        def _():
            copy(r).wait()

    @pl.when(count > 0)
    def _():
        arrived(0)
        for n in range(PAIRS):
            phase1(0, todo[0], n, bufa)
        def rows(p, c):
            arrived(2 * p + 1)
            both(2 * p + 1, bufb, 2 * p, bufa)
            arrived(2 * p + 2)
            both(2 * p + 2, bufa, 2 * p + 1, bufb)
            return c
        lax.fori_loop(0, (count + 1) // 2, rows, 0)

    gf = 18 if chunks == 1 else 14
    gh = gf // 2
    def gathered(t2, u, each, groups):
        cols_ = []
        for n in range(each):
            rows_ = []
            for g in range(groups):
                at = pl.multiple_of((t2 + g * each + n) * B + 8 * u, 8)
                rows_.append(lo[pl.ds(at, 8), :] + hi[pl.ds(at, 8), :])
            cols_.append(jnp.concatenate(rows_, axis=0).astype(bf))
        return jnp.concatenate(cols_, axis=1)
    def flush(b, c):
        t2 = b * (gf * 4)
        for y, u in enumerate(FULL):
            x = jnp.dot(gathered(t2, u, 4, gf), full_ref[...], preferred_element_type=f32)
            for g in range(gf):
                for w in range(3):
                    at = pl.multiple_of(((b * gf + g) * 3 + w) * 128, 128)
                    out[y, :, pl.ds(at, 128)] = x[8 * g:8 * g + 8, w * 128:w * 128 + 128].astype(bf)
        for u in (1, 4):
            x0 = gathered(t2, u, 8, gh)
            for y, (v, h) in enumerate(SPLIT):
                if v == u:
                    x = jnp.dot(x0, half_ref[h], preferred_element_type=f32)
                    for g in range(gh):
                        for w in range(3):
                            at = pl.multiple_of((total * B // 128 + (b * gh + g) * 3 + w) * 128, 128)
                            out[y, :, pl.ds(at, 128)] = x[8 * g:8 * g + 8, w * 128:w * 128 + 128].astype(bf)
        return c
    lax.fori_loop(0, total // (8 * gf), flush, 0)
    away = [pltpu.make_async_copy(out.at[(here[0] + d) & 3], sends[d], osems.at[d]) for d in range(4)]
    for c in away:
        c.start()
    for c in away:
        c.wait()
    if keeps:
        keep.wait()

def main(q, chunks, colsT, slotsT, agg, here, blocks, turned, pieces):
    hbm = pl.BlockSpec(memory_space=pl.ANY)
    crows, kslots = slots_of(chunks)
    total = crows * kslots
    shape = [jax.ShapeDtypeStruct((8, total * 72), bf)] * 4 + [jax.ShapeDtypeStruct((TILE, 128), bf)] * (q == 0 and chunks > 1)
    return pl.pallas_call(
        functools.partial(main_kernel, q, chunks),
        out_shape=shape,
        in_specs=[pl.BlockSpec(memory_space=pltpu.SMEM)] * 4 + [hbm] * (2 + len(pieces)),
        out_specs=[hbm] * len(shape),
        scratch_shapes=[pltpu.VMEM((4, 8, total * 72), bf), pltpu.SemaphoreType.DMA((4,)), pltpu.VMEM((R, K, B, B), bf), pltpu.VMEM((R, B, B), bf), pltpu.VMEM((2 * TILE, 128), bf)]
            + [pltpu.VMEM(((total // 2 + 1) * B, 128), f32)] * 2 + [pltpu.VMEM((B, PAIRS * 256), bf)] * 2
            + [pltpu.VMEM((32, 128), bf), pltpu.VMEM((512, 384), bf), pltpu.VMEM((2, 1024, 384), bf)]
            + [pltpu.SMEM((R + 1,), jnp.int32), pltpu.SemaphoreType.DMA((R,)), pltpu.SemaphoreType.DMA((len(pieces) + 1,))],
        compiler_params=pltpu.CompilerParams(vmem_limit_bytes=60 << 20),
        cost_estimate=pl.CostEstimate(flops=2 * 10**10 // chunks, bytes_accessed=10**7, transcendentals=0),
    )(colsT, slotsT, agg, here, blocks, turned, *pieces)

def chunk_rows(chunks):
    crows, kslots = slots_of(chunks)
    rows = crows * kslots * 72 // 128
    return rows, -(-rows // 16) * 16

def sum_kernel(chunks, *refs):
    o_ref, buf = refs[-2:]
    rows, padded = chunk_rows(chunks)
    each = chunks * padded
    for q in range(chunks):
        x = refs[4 * q:4 * q + 4]
        def body(b, c):
            at = pl.multiple_of(b * 128, 128)
            s = (x[0][:, pl.ds(at, 128)].astype(f32) + x[1][:, pl.ds(at, 128)].astype(f32)) + (
                x[2][:, pl.ds(at, 128)].astype(f32) + x[3][:, pl.ds(at, 128)].astype(f32))
            buf[pl.ds(q * padded + b, 8, stride=each), :] = s
            return c
        lax.fori_loop(0, rows, body, 0, unroll=9)
    for z in range(8):
        o_ref[z] = buf[z * each:(z + 1) * each, :].astype(bf)

def sum_y(chunks, parts):
    each = chunks * chunk_rows(chunks)[1]
    return pl.pallas_call(functools.partial(sum_kernel, chunks), out_shape=jax.ShapeDtypeStruct((8, each, 128), bf),
                          scratch_shapes=[pltpu.VMEM((8 * each, 128), f32)])(*parts)

def final_kernel(chunks, par_ref, x_ref, o_ref, tot):
    crows, kslots = slots_of(chunks)
    total = crows * kslots
    padded = chunk_rows(chunks)[1]
    tot[...] = functools.reduce(lambda p, q: p + q, [x_ref[z].astype(f32) for z in range(8)])
    odd = par_ref[0]
    l0 = lax.broadcasted_iota(jnp.int32, (384, 128), 0)
    l1 = lax.broadcasted_iota(jnp.int32, (384, 128), 1)
    for q in range(chunks):
        acc = jnp.zeros((total, 128), f32)
        for step, start, place in ((B, 0, odd * HALF), (HALF, total * B // 128, (1 - odd) * B)):
            side = 384 // step
            groups = total // side
            pick = (l0 % step + place == l1).astype(f32).astype(bf)
            lane = lax.broadcasted_iota(jnp.int32, (1, side, 128), 2)
            which = lax.broadcasted_iota(jnp.int32, (1, side, 128), 1)
            xs = [tot[pl.ds(q * padded + start + w, groups, stride=3), :] for w in range(3)]
            for _ in range(3):
                wide = []
                for w in range(3):
                    top = xs[w].astype(bf).astype(f32)
                    xs[w] = xs[w] - top
                    mine = (lane + w * 128) // step == which
                    wide.append(jnp.where(mine, top[:, None, :], 0.0).reshape(total, 128).astype(bf))
                acc = acc + jnp.dot(jnp.concatenate(wide, axis=1), pick, preferred_element_type=f32)
        o_ref[:, q * crows:(q + 1) * crows, :] = acc[:KC * crows, :72].reshape(KC, crows, 72)

def final(chunks, par, x):
    each = chunks * chunk_rows(chunks)[1]
    return pl.pallas_call(functools.partial(final_kernel, chunks), out_shape=jax.ShapeDtypeStruct((KC, CR, 72), f32),
                          in_specs=[pl.BlockSpec(memory_space=pltpu.SMEM), pl.BlockSpec(memory_space=pltpu.VMEM)],
                          scratch_shapes=[pltpu.VMEM((each, 128), f32)])(par, x)

CHUNKS = 2
ZG = [[z * 4 + y for z in range(8)] for y in range(4)]

def gather(p):
    def along(by):
        return lax.ppermute(p, "row", [(i, (i + 2 * by) % 8) for i in range(8)])
    def across(x):
        return lax.ppermute(x, "row", [(i, i ^ 1) for i in range(8)])
    mine = [p, along(-1), along(1), along(2)]
    return mine + [across(q) for q in mine]

def places(columns):
    row = lax.axis_index("row")
    owner = columns // R
    apart = ((owner >> 1) - (row >> 1)) & 3
    at = jnp.where(apart == 3, 2, jnp.where(apart == 2, 3, apart)) + 4 * ((owner ^ row) & 1)
    return at * R + columns % R

def shards(blocks, prolong, columns, aggregate, slots):
    turned = turn(prolong)
    pieces = gather(pack(prolong))
    cols = places(columns).T
    y = lax.axis_index("col") & 3
    parts = []
    for q in range(CHUNKS):
        out = main(q, CHUNKS, cols, slots.T, aggregate, y.reshape(1), blocks, turned, pieces)
        if q == 0:
            pieces = pieces + list(out[4:])
        if q:
            parts, out = lax.optimization_barrier((parts, out))
            parts, out = list(parts), list(out)
        parts.append(out[0])
        for d in range(1, 4):
            parts.append(lax.ppermute(out[d], "col", [(4 * z + k, 4 * z + (k + d) % 4) for z in range(8) for k in range(4)]))
    summed = lax.all_to_all(sum_y(CHUNKS, parts), "col", 0, 0, axis_index_groups=ZG, tiled=True)
    return final(CHUNKS, (y & 1).reshape(1), summed).transpose(1, 0, 2)


def solution(mesh):
    return jax.shard_map(
        shards,
        mesh=mesh,
        in_specs=(
            jax.sharding.PartitionSpec(("row", "col"), None, None, None),
            jax.sharding.PartitionSpec(("row", "col"), None, None),
            jax.sharding.PartitionSpec(("row", "col"), None),
            jax.sharding.PartitionSpec(("row", "col")),
            jax.sharding.PartitionSpec(("row", "col"), None),
        ),
        out_specs=jax.sharding.PartitionSpec("row", None, "col"),
        check_vma=False,
    )
```

```python
import functools
import jax, jax.numpy as jnp
from jax import lax
from jax.experimental import pallas as pl
from jax.experimental.pallas import tpu as pltpu
bf, f32 = jnp.bfloat16, jnp.float32
B, K, KC, CR, R = 48, 27, 27, 16, 48
PAIRS = (K + 1) // 2
PIECE = R // 2 * B
HALF = B // 2
TILE = 8 * PIECE
FULL = (0, 2, 3, 5)
SPLIT = ((1, 0), (1, 1), (4, 0), (4, 1))

T = KC * CR
FIRST = 288
REST = T - FIRST
ROWS1 = FIRST * 72 // 128
PAD1 = 176
ROWS2 = REST * 72 // 128
PAD2 = 88

def pack_kernel(p_ref, o_ref):
    pad = jnp.zeros((B, 128 - 2 * B), bf)
    for n in range(R // 2):
        o_ref[n * B:(n + 1) * B, :] = jnp.concatenate([p_ref[2 * n], p_ref[2 * n + 1], pad], axis=1)

def pack(p):
    return pl.pallas_call(pack_kernel, out_shape=jax.ShapeDtypeStruct((PIECE, 128), bf))(p)

def turn_kernel(p_ref, o_ref):
    row = lax.broadcasted_iota(jnp.int32, (B, B), 0)
    a = lax.broadcasted_iota(jnp.int32, (B, B), 1)
    pick = (row == (a % 6) * 8 + a // 6).astype(f32).astype(bf)
    for i in range(R):
        o_ref[i] = lax.dot_general(pick, p_ref[i], (((1,), (1,)), ((), ())), preferred_element_type=f32).astype(bf)

def turn(p):
    return pl.pallas_call(turn_kernel, out_shape=jax.ShapeDtypeStruct((R, B, B), bf),
                          cost_estimate=pl.CostEstimate(flops=10**7, bytes_accessed=2 * 10**6, transcendentals=0))(p)

def place_kernel_matrix(n, step, off):
    row = lax.broadcasted_iota(jnp.int32, (n * 128, 384), 0)
    col = lax.broadcasted_iota(jnp.int32, (n * 128, 384), 1)
    t, c = col // step, col % step
    return (row == (t // 2) * 128 + (t % 2) * B + off + c).astype(f32).astype(bf)

def main_kernel(src, odd, dst, here, blk_hbm, turned_hbm, *rest):
    pieces, sends, out2, (out, buf2, osems, blk, turned, tile, lo, hi, bufa, bufb, only, full_ref, half_ref, sems, psems) = (
        rest[:8], rest[8:12], rest[12], rest[13:])
    first = [pltpu.make_async_copy(piece, tile.at[pl.ds(n * PIECE, PIECE)], psems.at[n]) for n, piece in enumerate(pieces)]
    first.append(pltpu.make_async_copy(turned_hbm, turned, psems.at[8]))
    CH = 4
    def copy(n):
        return pltpu.make_async_copy(blk_hbm.at[pl.ds(n * CH, CH)], blk.at[pl.ds(n * CH, CH)], sems.at[n])
    for c in first:
        c.start()
    for n in range(R // CH):
        copy(n).start()

    def zero(n, c):
        z = pl.multiple_of(n * 384, 8)
        lo[pl.ds(z, 384), :] = jnp.zeros((384, 128), f32)
        hi[pl.ds(z, 384), :] = jnp.zeros((384, 128), f32)
        return c
    lax.fori_loop(0, T // 2 * B // 384, zero, 0)
    lane = lax.broadcasted_iota(jnp.int32, (32, 128), 1)
    row = lax.broadcasted_iota(jnp.int32, (32, 128), 0)
    only[...] = ((lane >= B * (row // 16)) & (lane < B * (row // 16) + B)).astype(f32).astype(bf)
    full_ref[...] = place_kernel_matrix(4, B, 0)
    for h in range(2):
        half_ref[h] = place_kernel_matrix(8, HALF, h * HALF)

    l0 = lax.broadcasted_iota(jnp.int32, (128, 128), 0)
    l1 = lax.broadcasted_iota(jnp.int32, (128, 128), 1)
    change = ((l0 < 2 * B) & (l1 == jnp.where(l0 < B, l0 + B, l0 - B))).astype(f32).astype(bf)
    for n in range(8):
        first[n].wait()
        tile[TILE + n * PIECE:TILE + (n + 1) * PIECE, :] = jnp.dot(
            tile[n * PIECE:(n + 1) * PIECE, :], change, preferred_element_type=f32).astype(bf)
    first[8].wait()

    def phase1(i, n, buf):
        ks = list(range(2 * n, min(2 * n + 2, K)))
        w = []
        for k in ks:
            mask = only[pl.ds(pl.multiple_of(odd[k, i], 16), 16), :]
            w.append(tile[pl.ds(pl.multiple_of(src[k, i], B), B), :] * jnp.concatenate([mask] * 3, axis=0))
        if len(ks) == 2:
            none = jnp.zeros((B, 128), bf)
            lhs = jnp.concatenate([blk[i, ks[0]], blk[i, ks[1]]], axis=1)
            w = jnp.concatenate([jnp.concatenate([w[0], none], axis=1), jnp.concatenate([none, w[1]], axis=1)], axis=0)
            buf[:, n * 256:(n + 1) * 256] = jnp.dot(lhs, w, preferred_element_type=f32).astype(bf)
        else:
            buf[:, n * 256:n * 256 + 128] = jnp.dot(blk[i, ks[0]], w[0], preferred_element_type=f32).astype(bf)

    def phase2(i, n, buf):
        wide = 256 if 2 * n + 1 < K else 128
        term = jnp.dot(turned[i], buf[:, n * 256:n * 256 + wide], preferred_element_type=f32)
        for m in range(wide // 128):
            k = 2 * n + m
            acc = hi if m & 1 else lo
            acc[pl.ds(pl.multiple_of(dst[k, i], B), B), :] += term[:, m * 128:(m + 1) * 128]

    def both(i1, buf1, i2, buf2):
        for n in range(PAIRS):
            phase2(i2, n, buf2)
            phase1(i1, n, buf1)

    copy(0).wait()
    for n in range(PAIRS):
        phase1(0, n, bufa)
    def rows(p, c):
        both(2 * p + 1, bufb, 2 * p, bufa)
        @pl.when((p & 1 == 1) & (p < R // 2 - 1))
        def _():
            copy((p + 1) // 2).wait()
        both(jnp.minimum(2 * p + 2, R - 1), bufa, 2 * p + 1, bufb)
        return c
    lax.fori_loop(0, R // 2, rows, 0)

    def gathered(t2, u, each, groups):
        cols_ = []
        for n in range(each):
            rows_ = []
            for g in range(groups):
                at = (t2 + g * each + n) * B + 8 * u
                rows_.append(lo[at:at + 8, :] + hi[at:at + 8, :])
            cols_.append(jnp.concatenate(rows_, axis=0).astype(bf))
        return jnp.concatenate(cols_, axis=1)
    gf, gh = 18, 9
    def put(b, y, half, x):
        for g in range(gh if half else gf):
            for w in range(3):
                v = x[8 * g:8 * g + 8, w * 128:w * 128 + 128]
                if b < 2:
                    at = ((FIRST * B // 128 if half else 0) + (b * (gh if half else gf) + g) * 3 + w) * 128
                    out[y, :, at:at + 128] = v.astype(bf)
                else:
                    r = y * PAD2 + (REST * B // 128 if half else 0) + g * 3 + w
                    buf2[pl.ds(r, 8, stride=4 * PAD2), :] = v
    away = [pltpu.make_async_copy(out.at[(here[0] + d) & 3], sends[d], osems.at[d]) for d in range(4)]
    for b in range(3):
        t2 = b * (gf * 4)
        for y, u in enumerate(FULL):
            put(b, y, False, jnp.dot(gathered(t2, u, 4, gf), full_ref[...], preferred_element_type=f32))
        for u in (1, 4):
            x0 = gathered(t2, u, 8, gh)
            for y, (v, h) in enumerate(SPLIT):
                if v == u:
                    put(b, y, True, jnp.dot(x0, half_ref[h], preferred_element_type=f32))
        if b == 1:
            for c in away:
                c.start()
    for z in range(8):
        out2[z] = buf2[z * 4 * PAD2:(z + 1) * 4 * PAD2, :].astype(bf)
    for c in away:
        c.wait()

def main(src, odd, dst, here, blocks, turned, pieces):
    hbm = pl.BlockSpec(memory_space=pl.ANY)
    vmem = pl.BlockSpec(memory_space=pltpu.VMEM)
    return pl.pallas_call(
        main_kernel,
        out_shape=[jax.ShapeDtypeStruct((8, FIRST * 72), bf)] * 4 + [jax.ShapeDtypeStruct((8, 4 * PAD2, 128), bf)],
        in_specs=[pl.BlockSpec(memory_space=pltpu.SMEM)] * 4 + [hbm] * 10,
        out_specs=[hbm] * 4 + [vmem],
        scratch_shapes=[pltpu.VMEM((4, 8, FIRST * 72), bf), pltpu.VMEM((8 * 4 * PAD2, 128), f32), pltpu.SemaphoreType.DMA((4,)),
                        pltpu.VMEM((R, K, B, B), bf), pltpu.VMEM((R, B, B), bf), pltpu.VMEM((2 * TILE, 128), bf)]
            + [pltpu.VMEM((T // 2 * B, 128), f32)] * 2 + [pltpu.VMEM((B, PAIRS * 256), bf)] * 2
            + [pltpu.VMEM((32, 128), bf), pltpu.VMEM((512, 384), bf), pltpu.VMEM((2, 1024, 384), bf)]
            + [pltpu.SemaphoreType.DMA((12,)), pltpu.SemaphoreType.DMA((9,))],
        compiler_params=pltpu.CompilerParams(vmem_limit_bytes=58 << 20),
        cost_estimate=pl.CostEstimate(flops=2 * 10**10, bytes_accessed=10**7, transcendentals=0),
    )(src, odd, dst, here, blocks, turned, *pieces)

def sum_y_kernel(x0, x1, x2, x3, o_ref, buf):
    def body(b, c):
        at = pl.multiple_of(b * 128, 128)
        s = (x0[:, pl.ds(at, 128)].astype(f32) + x1[:, pl.ds(at, 128)].astype(f32)) + (
            x2[:, pl.ds(at, 128)].astype(f32) + x3[:, pl.ds(at, 128)].astype(f32))
        buf[pl.ds(b, 8, stride=PAD1), :] = s
        return c
    lax.fori_loop(0, ROWS1, body, 0, unroll=18)
    for z in range(8):
        o_ref[z] = buf[z * PAD1:(z + 1) * PAD1, :].astype(bf)

def sum_y(parts):
    return pl.pallas_call(sum_y_kernel, out_shape=jax.ShapeDtypeStruct((8, PAD1, 128), bf),
                          scratch_shapes=[pltpu.VMEM((8 * PAD1, 128), f32)])(*parts)

def sum_z_kernel(here, x_ref, *refs):
    outs, tot = refs[:4], refs[4]
    tot[...] = functools.reduce(lambda p, q: p + q, [x_ref[z].astype(f32) for z in range(8)])
    for d in range(4):
        outs[d][...] = tot[pl.ds(pl.multiple_of(((here[0] + d) & 3) * PAD2, 8), PAD2), :].astype(bf)

def sum_z(here, x):
    return pl.pallas_call(sum_z_kernel, out_shape=[jax.ShapeDtypeStruct((PAD2, 128), bf)] * 4,
                          in_specs=[pl.BlockSpec(memory_space=pltpu.SMEM), pl.BlockSpec(memory_space=pltpu.VMEM)],
                          scratch_shapes=[pltpu.VMEM((4 * PAD2, 128), f32)])(here, x)

def final_kernel(here, x_ref, y0, y1, y2, y3, o_ref, tot1, tot2):
    tot1[...] = functools.reduce(lambda p, q: p + q, [x_ref[z].astype(f32) for z in range(8)])
    tot2[...] = functools.reduce(lambda p, q: p + q, [y[...].astype(f32) for y in (y0, y1, y2, y3)])
    odd = here[0] & 1
    l0 = lax.broadcasted_iota(jnp.int32, (384, 128), 0)
    l1 = lax.broadcasted_iota(jnp.int32, (384, 128), 1)
    for tot, total, slot in ((tot1, FIRST, 0), (tot2, REST, FIRST // CR)):
        acc = jnp.zeros((total, 128), f32)
        for step, start, place in ((B, 0, odd * HALF), (HALF, total * B // 128, (1 - odd) * B)):
            side = 384 // step
            groups = total // side
            pick = (l0 % step + place == l1).astype(f32).astype(bf)
            lane = lax.broadcasted_iota(jnp.int32, (1, side, 128), 2)
            which = lax.broadcasted_iota(jnp.int32, (1, side, 128), 1)
            xs = [tot[pl.ds(start + w, groups, stride=3), :] for w in range(3)]
            for _ in range(3):
                wide = []
                for w in range(3):
                    top = xs[w].astype(bf).astype(f32)
                    xs[w] = xs[w] - top
                    mine = (lane + w * 128) // step == which
                    wide.append(jnp.where(mine, top[:, None, :], 0.0).reshape(total, 128).astype(bf))
                acc = acc + jnp.dot(jnp.concatenate(wide, axis=1), pick, preferred_element_type=f32)
        o_ref[slot:slot + total // CR] = acc[:, :72].reshape(total // CR, CR, 72)

def final(here, x, parts):
    return pl.pallas_call(final_kernel, out_shape=jax.ShapeDtypeStruct((KC, CR, 72), f32),
                          in_specs=[pl.BlockSpec(memory_space=pltpu.SMEM)] + [pl.BlockSpec(memory_space=pltpu.VMEM)] * 5,
                          scratch_shapes=[pltpu.VMEM((PAD1, 128), f32), pltpu.VMEM((PAD2, 128), f32)])(here, x, *parts)

ZG = [[z * 4 + y for z in range(8)] for y in range(4)]

def along_x(x, by):
    return lax.ppermute(x, "row", [(i, (i + 2 * by) % 8) for i in range(8)])

def across(x):
    return lax.ppermute(x, "row", [(i, i ^ 1) for i in range(8)])

def along_y(x, by):
    return lax.ppermute(x, "col", [(4 * z + y, 4 * z + (y + by) % 4) for z in range(8) for y in range(4)])

def exchange_z(x):
    return lax.all_to_all(x, "col", 0, 0, axis_index_groups=ZG, tiled=True)

def indices(columns, aggregate, slots):
    row = lax.axis_index("row")
    owner = columns // R
    apart = ((owner >> 1) - (row >> 1)) & 3
    j = (jnp.where(apart == 3, 2, jnp.where(apart == 2, 3, apart)) + 4 * ((owner ^ row) & 1)) * R + columns % R
    target = slots * CR + aggregate[:, None]
    odd = target & 1
    return ((j >> 1) * B + ((j ^ odd) & 1) * TILE).T, (odd * 16).T, ((target >> 1) * B).T

def shards(blocks, prolong, columns, aggregate, slots):
    packed = pack(prolong)
    mine = [packed, along_x(packed, -1), along_x(packed, 1), along_x(packed, 2)]
    index = indices(columns, aggregate, slots)
    turned = turn(prolong)
    *near, turned, index = lax.optimization_barrier((*mine, turned, index))
    pieces = near + [across(x) for x in near]
    here = (lax.axis_index("col") & 3).reshape(1)
    *sends, other = main(*index, here, blocks, turned, pieces)
    parts = [sends[0]] + [along_y(sends[d], d) for d in range(1, 4)]
    other = sum_z(here, exchange_z(other))
    first = exchange_z(sum_y(parts))
    other = [other[0]] + [along_y(other[d], d) for d in range(1, 4)]
    return final(here, first, other).transpose(1, 0, 2)


def solution(mesh):
    return jax.shard_map(
        shards,
        mesh=mesh,
        in_specs=(
            jax.sharding.PartitionSpec(("row", "col"), None, None, None),
            jax.sharding.PartitionSpec(("row", "col"), None, None),
            jax.sharding.PartitionSpec(("row", "col"), None),
            jax.sharding.PartitionSpec(("row", "col")),
            jax.sharding.PartitionSpec(("row", "col"), None),
        ),
        out_specs=jax.sharding.PartitionSpec("row", None, "col"),
        check_vma=False,
    )
```

```python
import functools
import jax, jax.numpy as jnp
from jax import lax
from jax.experimental import pallas as pl
from jax.experimental.pallas import tpu as pltpu
bf, f32 = jnp.bfloat16, jnp.float32
B, K, KC, CR, R = 48, 27, 27, 16, 48
PAIRS = (K + 1) // 2
PIECE = R // 2 * B
HALF = B // 2
TILE = 8 * PIECE
FULL = (0, 2, 3, 5)
SPLIT = ((1, 0), (1, 1), (4, 0), (4, 1))

T = KC * CR
FIRST = 288
REST = T - FIRST
ROWS1 = FIRST * 72 // 128
PAD1 = 176
ROWS2 = REST * 72 // 128
PAD2 = 88

def pack_kernel(p_ref, o_ref):
    for g in range(R // 8):
        o_ref[g * B:(g + 1) * B, :] = jnp.concatenate([p_ref[8 * g + m] for m in range(8)], axis=1)

def pack(p):
    return pl.pallas_call(pack_kernel, out_shape=jax.ShapeDtypeStruct((R // 8 * B, 8 * B), bf))(p)

def turn_kernel(p_ref, o_ref):
    row = lax.broadcasted_iota(jnp.int32, (B, B), 0)
    a = lax.broadcasted_iota(jnp.int32, (B, B), 1)
    pick = (row == (a % 6) * 8 + a // 6).astype(f32).astype(bf)
    for i in range(R):
        o_ref[i] = lax.dot_general(pick, p_ref[i], (((1,), (1,)), ((), ())), preferred_element_type=f32).astype(bf)

def turn(p):
    return pl.pallas_call(turn_kernel, out_shape=jax.ShapeDtypeStruct((R, B, B), bf),
                          cost_estimate=pl.CostEstimate(flops=10**7, bytes_accessed=2 * 10**6, transcendentals=0))(p)

def place_kernel_matrix(n, step, off):
    row = lax.broadcasted_iota(jnp.int32, (n * 128, 384), 0)
    col = lax.broadcasted_iota(jnp.int32, (n * 128, 384), 1)
    t, c = col // step, col % step
    return (row == (t // 2) * 128 + (t % 2) * B + off + c).astype(f32).astype(bf)

def main_kernel(src, odd, dst, here, blk_hbm, turned_hbm, *rest):
    pieces, sends, out2, (stage, out, buf2, osems, blk, turned, tile, lo, hi, bufa, bufb, only, full_ref, half_ref, sems, psems) = (
        rest[:8], rest[8:12], rest[12], rest[13:])
    first = [pltpu.make_async_copy(piece, stage.at[n], psems.at[n]) for n, piece in enumerate(pieces)]
    first.append(pltpu.make_async_copy(turned_hbm, turned, psems.at[8]))
    CH = 4
    def copy(n):
        return pltpu.make_async_copy(blk_hbm.at[pl.ds(n * CH, CH)], blk.at[pl.ds(n * CH, CH)], sems.at[n])
    for c in first:
        c.start()
    for n in range(R // CH):
        copy(n).start()

    def zero(n, c):
        z = pl.multiple_of(n * 384, 8)
        lo[pl.ds(z, 384), :] = jnp.zeros((384, 128), f32)
        hi[pl.ds(z, 384), :] = jnp.zeros((384, 128), f32)
        return c
    lax.fori_loop(0, T // 2 * B // 384, zero, 0)
    lane = lax.broadcasted_iota(jnp.int32, (32, 128), 1)
    row = lax.broadcasted_iota(jnp.int32, (32, 128), 0)
    only[...] = ((lane >= B * (row // 16)) & (lane < B * (row // 16) + B)).astype(f32).astype(bf)
    full_ref[...] = place_kernel_matrix(4, B, 0)
    for h in range(2):
        half_ref[h] = place_kernel_matrix(8, HALF, h * HALF)

    picks = []
    for p in range(4):
        start = 2 * B * p // 128 * 128
        wide = min(256, 8 * B - start)
        l0 = lax.broadcasted_iota(jnp.int32, (wide, 256), 0) + start - 2 * B * p
        l1 = lax.broadcasted_iota(jnp.int32, (wide, 256), 1)
        other = l1 - 128
        keep = (l1 < 2 * B) & (l0 == l1)
        change = (other >= 0) & (other < 2 * B) & (l0 == jnp.where(other < B, other + B, other - B))
        picks.append((start, wide, (keep | change).astype(f32).astype(bf)))
    for n in range(8):
        first[n].wait()
        for p, (start, wide, pick) in enumerate(picks):
            x = jnp.dot(stage[n, :, start:start + wide], pick, preferred_element_type=f32).astype(bf)
            at = (4 * n + p) * (R // 8 * B)
            tile[at:at + R // 8 * B, :] = x[:, :128]
            tile[TILE + at:TILE + at + R // 8 * B, :] = x[:, 128:]
    first[8].wait()

    def phase1(i, n, buf):
        ks = list(range(2 * n, min(2 * n + 2, K)))
        w = []
        for k in ks:
            mask = only[pl.ds(pl.multiple_of(odd[k, i], 16), 16), :]
            w.append(tile[pl.ds(pl.multiple_of(src[k, i], B), B), :] * jnp.concatenate([mask] * 3, axis=0))
        if len(ks) == 2:
            none = jnp.zeros((B, 128), bf)
            lhs = jnp.concatenate([blk[i, ks[0]], blk[i, ks[1]]], axis=1)
            w = jnp.concatenate([jnp.concatenate([w[0], none], axis=1), jnp.concatenate([none, w[1]], axis=1)], axis=0)
            buf[:, n * 256:(n + 1) * 256] = jnp.dot(lhs, w, preferred_element_type=f32).astype(bf)
        else:
            buf[:, n * 256:n * 256 + 128] = jnp.dot(blk[i, ks[0]], w[0], preferred_element_type=f32).astype(bf)

    def phase2(i, n, buf):
        wide = 256 if 2 * n + 1 < K else 128
        term = jnp.dot(turned[i], buf[:, n * 256:n * 256 + wide], preferred_element_type=f32)
        for m in range(wide // 128):
            k = 2 * n + m
            acc = hi if m & 1 else lo
            acc[pl.ds(pl.multiple_of(dst[k, i], B), B), :] += term[:, m * 128:(m + 1) * 128]

    def both(i1, buf1, i2, buf2):
        for n in range(PAIRS):
            phase2(i2, n, buf2)
            phase1(i1, n, buf1)

    copy(0).wait()
    for n in range(PAIRS):
        phase1(0, n, bufa)
    def rows(p, c):
        both(2 * p + 1, bufb, 2 * p, bufa)
        @pl.when((p & 1 == 1) & (p < R // 2 - 1))
        def _():
            copy((p + 1) // 2).wait()
        both(jnp.minimum(2 * p + 2, R - 1), bufa, 2 * p + 1, bufb)
        return c
    lax.fori_loop(0, R // 2, rows, 0)

    def gathered(t2, u, each, groups):
        cols_ = []
        for n in range(each):
            rows_ = []
            for g in range(groups):
                at = (t2 + g * each + n) * B + 8 * u
                rows_.append(lo[at:at + 8, :] + hi[at:at + 8, :])
            cols_.append(jnp.concatenate(rows_, axis=0).astype(bf))
        return jnp.concatenate(cols_, axis=1)
    gf, gh = 18, 9
    def put(b, y, half, x):
        for g in range(gh if half else gf):
            for w in range(3):
                v = x[8 * g:8 * g + 8, w * 128:w * 128 + 128]
                if b < 2:
                    at = ((FIRST * B // 128 if half else 0) + (b * (gh if half else gf) + g) * 3 + w) * 128
                    out[y, :, at:at + 128] = v.astype(bf)
                else:
                    r = y * PAD2 + (REST * B // 128 if half else 0) + g * 3 + w
                    buf2[pl.ds(r, 8, stride=4 * PAD2), :] = v
    away = [pltpu.make_async_copy(out.at[(here[0] + d) & 3], sends[d], osems.at[d]) for d in range(4)]
    for b in range(3):
        t2 = b * (gf * 4)
        for y, u in enumerate(FULL):
            put(b, y, False, jnp.dot(gathered(t2, u, 4, gf), full_ref[...], preferred_element_type=f32))
        for u in (1, 4):
            x0 = gathered(t2, u, 8, gh)
            for y, (v, h) in enumerate(SPLIT):
                if v == u:
                    put(b, y, True, jnp.dot(x0, half_ref[h], preferred_element_type=f32))
        if b == 1:
            for c in away:
                c.start()
    for z in range(8):
        out2[z] = buf2[z * 4 * PAD2:(z + 1) * 4 * PAD2, :].astype(bf)
    for c in away:
        c.wait()

def main(src, odd, dst, here, blocks, turned, pieces):
    hbm = pl.BlockSpec(memory_space=pl.ANY)
    vmem = pl.BlockSpec(memory_space=pltpu.VMEM)
    return pl.pallas_call(
        main_kernel,
        out_shape=[jax.ShapeDtypeStruct((8, FIRST * 72), bf)] * 4 + [jax.ShapeDtypeStruct((8, 4 * PAD2, 128), bf)],
        in_specs=[pl.BlockSpec(memory_space=pltpu.SMEM)] * 4 + [hbm] * 10,
        out_specs=[hbm] * 4 + [vmem],
        scratch_shapes=[pltpu.VMEM((8, R // 8 * B, 8 * B), bf), pltpu.VMEM((4, 8, FIRST * 72), bf), pltpu.VMEM((8 * 4 * PAD2, 128), f32), pltpu.SemaphoreType.DMA((4,)),
                        pltpu.VMEM((R, K, B, B), bf), pltpu.VMEM((R, B, B), bf), pltpu.VMEM((2 * TILE, 128), bf)]
            + [pltpu.VMEM((T // 2 * B, 128), f32)] * 2 + [pltpu.VMEM((B, PAIRS * 256), bf)] * 2
            + [pltpu.VMEM((32, 128), bf), pltpu.VMEM((512, 384), bf), pltpu.VMEM((2, 1024, 384), bf)]
            + [pltpu.SemaphoreType.DMA((12,)), pltpu.SemaphoreType.DMA((9,))],
        compiler_params=pltpu.CompilerParams(vmem_limit_bytes=58 << 20),
        cost_estimate=pl.CostEstimate(flops=2 * 10**10, bytes_accessed=10**7, transcendentals=0),
    )(src, odd, dst, here, blocks, turned, *pieces)

def sum_y_kernel(x0, x1, x2, x3, o_ref, buf):
    def body(b, c):
        at = pl.multiple_of(b * 128, 128)
        s = (x0[:, pl.ds(at, 128)].astype(f32) + x1[:, pl.ds(at, 128)].astype(f32)) + (
            x2[:, pl.ds(at, 128)].astype(f32) + x3[:, pl.ds(at, 128)].astype(f32))
        buf[pl.ds(b, 8, stride=PAD1), :] = s
        return c
    lax.fori_loop(0, ROWS1, body, 0, unroll=18)
    for z in range(8):
        o_ref[z] = buf[z * PAD1:(z + 1) * PAD1, :].astype(bf)

def sum_y(parts):
    return pl.pallas_call(sum_y_kernel, out_shape=jax.ShapeDtypeStruct((8, PAD1, 128), bf),
                          scratch_shapes=[pltpu.VMEM((8 * PAD1, 128), f32)],
                          cost_estimate=pl.CostEstimate(flops=4 * 10**10, bytes_accessed=10**7, transcendentals=0))(*parts)

def sum_z_kernel(here, x_ref, *refs):
    outs, tot = refs[:4], refs[4]
    tot[...] = functools.reduce(lambda p, q: p + q, [x_ref[z].astype(f32) for z in range(8)])
    for d in range(4):
        outs[d][...] = tot[pl.ds(pl.multiple_of(((here[0] + d) & 3) * PAD2, 8), PAD2), :].astype(bf)

def sum_z(here, x):
    return pl.pallas_call(sum_z_kernel, out_shape=[jax.ShapeDtypeStruct((PAD2, 128), bf)] * 4,
                          in_specs=[pl.BlockSpec(memory_space=pltpu.SMEM), pl.BlockSpec(memory_space=pltpu.VMEM)],
                          scratch_shapes=[pltpu.VMEM((4 * PAD2, 128), f32)])(here, x)

def final_kernel(here, x_ref, y0, y1, y2, y3, o_ref, tot1, tot2):
    tot1[...] = functools.reduce(lambda p, q: p + q, [x_ref[z].astype(f32) for z in range(8)])
    tot2[...] = functools.reduce(lambda p, q: p + q, [y[...].astype(f32) for y in (y0, y1, y2, y3)])
    odd = here[0] & 1
    l0 = lax.broadcasted_iota(jnp.int32, (384, 128), 0)
    l1 = lax.broadcasted_iota(jnp.int32, (384, 128), 1)
    for tot, total, slot in ((tot1, FIRST, 0), (tot2, REST, FIRST // CR)):
        acc = jnp.zeros((total, 128), f32)
        for step, start, place in ((B, 0, odd * HALF), (HALF, total * B // 128, (1 - odd) * B)):
            side = 384 // step
            groups = total // side
            pick = (l0 % step + place == l1).astype(f32).astype(bf)
            lane = lax.broadcasted_iota(jnp.int32, (1, side, 128), 2)
            which = lax.broadcasted_iota(jnp.int32, (1, side, 128), 1)
            xs = [tot[pl.ds(start + w, groups, stride=3), :] for w in range(3)]
            for _ in range(3):
                wide = []
                for w in range(3):
                    top = xs[w].astype(bf).astype(f32)
                    xs[w] = xs[w] - top
                    mine = (lane + w * 128) // step == which
                    wide.append(jnp.where(mine, top[:, None, :], 0.0).reshape(total, 128).astype(bf))
                acc = acc + jnp.dot(jnp.concatenate(wide, axis=1), pick, preferred_element_type=f32)
        o_ref[slot:slot + total // CR] = acc[:, :72].reshape(total // CR, CR, 72)

def final(here, x, parts):
    return pl.pallas_call(final_kernel, out_shape=jax.ShapeDtypeStruct((KC, CR, 72), f32),
                          in_specs=[pl.BlockSpec(memory_space=pltpu.SMEM)] + [pl.BlockSpec(memory_space=pltpu.VMEM)] * 5,
                          scratch_shapes=[pltpu.VMEM((PAD1, 128), f32), pltpu.VMEM((PAD2, 128), f32)])(here, x, *parts)

ZG = [[z * 4 + y for z in range(8)] for y in range(4)]

def along_x(x, by):
    return lax.ppermute(x, "row", [(i, (i + 2 * by) % 8) for i in range(8)])

def across(x):
    return lax.ppermute(x, "row", [(i, i ^ 1) for i in range(8)])

def along_y(x, by):
    return lax.ppermute(x, "col", [(4 * z + y, 4 * z + (y + by) % 4) for z in range(8) for y in range(4)])

def exchange_z(x):
    return lax.all_to_all(x, "col", 0, 0, axis_index_groups=ZG, tiled=True)

def indices(columns, aggregate, slots):
    row = lax.axis_index("row")
    owner = columns // R
    apart = ((owner >> 1) - (row >> 1)) & 3
    piece = jnp.where(apart == 3, 2, jnp.where(apart == 2, 3, apart)) + 4 * ((owner ^ row) & 1)
    t = columns % R
    at = piece * (R // 2) + ((t & 7) >> 1) * (R // 8) + (t >> 3)
    target = slots * CR + aggregate[:, None]
    odd = target & 1
    return (at * B + ((t ^ odd) & 1) * TILE).T, (odd * 16).T, ((target >> 1) * B).T

def shards(blocks, prolong, columns, aggregate, slots):
    packed = pack(prolong)
    mine = [packed, along_x(packed, -1), along_x(packed, 1), along_x(packed, 2)]
    index = indices(columns, aggregate, slots)
    turned = turn(prolong)
    *near, turned, index = lax.optimization_barrier((*mine, turned, index))
    pieces = near + [across(x) for x in near]
    here = (lax.axis_index("col") & 3).reshape(1)
    *sends, other = main(*index, here, blocks, turned, pieces)
    parts = [sends[0]] + [along_y(sends[d], d) for d in range(1, 4)]
    other = sum_z(here, exchange_z(other))
    first = exchange_z(sum_y(parts))
    other = [other[0]] + [along_y(other[d], d) for d in range(1, 4)]
    return final(here, first, other).transpose(1, 0, 2)


def solution(mesh):
    return jax.shard_map(
        shards,
        mesh=mesh,
        in_specs=(
            jax.sharding.PartitionSpec(("row", "col"), None, None, None),
            jax.sharding.PartitionSpec(("row", "col"), None, None),
            jax.sharding.PartitionSpec(("row", "col"), None),
            jax.sharding.PartitionSpec(("row", "col")),
            jax.sharding.PartitionSpec(("row", "col"), None),
        ),
        out_specs=jax.sharding.PartitionSpec("row", None, "col"),
        check_vma=False,
    )
```

```python
import functools
import jax, jax.numpy as jnp
from jax import lax
from jax.experimental import pallas as pl
from jax.experimental.pallas import tpu as pltpu
bf, f32 = jnp.bfloat16, jnp.float32
B, K, KC, CR, R = 48, 27, 27, 16, 48
PAIRS = (K + 1) // 2
PIECE = R // 2 * B
HALF = B // 2
TILE = 8 * PIECE
FULL = (0, 2, 3, 5)
SPLIT = ((1, 0), (1, 1), (4, 0), (4, 1))

T = KC * CR
FIRST = 336
REST = T - FIRST
ROWS1 = FIRST * 72 // 128
PAD1 = 192
ROWS2 = REST * 72 // 128
PAD2 = 56

def pack_kernel(p_ref, o_ref):
    for g in range(R // 8):
        o_ref[g * B:(g + 1) * B, :] = jnp.concatenate([p_ref[8 * g + m] for m in range(8)], axis=1)

def pack(p):
    return pl.pallas_call(pack_kernel, out_shape=jax.ShapeDtypeStruct((R // 8 * B, 8 * B), bf))(p)

def placing(n, step, off):
    row = lax.broadcasted_iota(jnp.int32, (n * 128, 384), 0)
    col = lax.broadcasted_iota(jnp.int32, (n * 128, 384), 1)
    t, c = col // step, col % step
    return (row == (t // 2) * 128 + (t % 2) * B + off + c).astype(f32).astype(bf)

def turn_kernel(p_ref, o_ref, full_ref, half_ref):
    row = lax.broadcasted_iota(jnp.int32, (B, B), 0)
    a = lax.broadcasted_iota(jnp.int32, (B, B), 1)
    pick = (row == (a % 6) * 8 + a // 6).astype(f32).astype(bf)
    for i in range(R):
        o_ref[i] = lax.dot_general(pick, p_ref[i], (((1,), (1,)), ((), ())), preferred_element_type=f32).astype(bf)
    full_ref[...] = placing(4, B, 0)
    for h in range(2):
        half_ref[h] = placing(8, HALF, h * HALF)

def turn(p):
    return pl.pallas_call(turn_kernel, out_shape=[jax.ShapeDtypeStruct((R, B, B), bf), jax.ShapeDtypeStruct((512, 384), bf),
                                                  jax.ShapeDtypeStruct((2, 1024, 384), bf)],
                          cost_estimate=pl.CostEstimate(flops=10**7, bytes_accessed=2 * 10**6, transcendentals=0))(p)

def main_kernel(src, odd, dst, here, blk_hbm, turned_hbm, full_hbm, half_hbm, *rest):
    pieces, sends, out2, (stage, out, buf2, osems, blk, turned, tile, lo, hi, bufa, bufb, only, full_ref, half_ref, sems, psems) = (
        rest[:8], rest[8:12], rest[12], rest[13:])
    first = [pltpu.make_async_copy(piece, stage.at[pl.ds(n * (R // 8 * B), R // 8 * B)], psems.at[n]) for n, piece in enumerate(pieces)]
    first.append(pltpu.make_async_copy(turned_hbm, turned, psems.at[8]))
    CH = 4
    def copy(n):
        return pltpu.make_async_copy(blk_hbm.at[pl.ds(n * CH, CH)], blk.at[pl.ds(n * CH, CH)], sems.at[n])
    late = [pltpu.make_async_copy(full_hbm, full_ref, psems.at[9]), pltpu.make_async_copy(half_hbm, half_ref, psems.at[10])]
    for c in first:
        c.start()
    for n in range(R // CH):
        copy(n).start()
    for c in late:
        c.start()

    def zero(n, c):
        z = pl.multiple_of(n * 384, 8)
        lo[pl.ds(z, 384), :] = jnp.zeros((384, 128), f32)
        hi[pl.ds(z, 384), :] = jnp.zeros((384, 128), f32)
        return c
    lax.fori_loop(0, T // 2 * B // 384, zero, 0)
    lane = lax.broadcasted_iota(jnp.int32, (32, 128), 1)
    row = lax.broadcasted_iota(jnp.int32, (32, 128), 0)
    only[...] = ((lane >= B * (row // 16)) & (lane < B * (row // 16) + B)).astype(f32).astype(bf)

    picks = []
    for p in range(4):
        start = 2 * B * p // 128 * 128
        wide = min(256, 8 * B - start)
        l0 = lax.broadcasted_iota(jnp.int32, (wide, 256), 0) + start - 2 * B * p
        l1 = lax.broadcasted_iota(jnp.int32, (wide, 256), 1)
        other = l1 - 128
        keep = (l1 < 2 * B) & (l0 == l1)
        change = (other >= 0) & (other < 2 * B) & (l0 == jnp.where(other < B, other + B, other - B))
        picks.append((start, wide, (keep | change).astype(f32).astype(bf)))
    side = R // 8 * B
    for q in range(2):
        for n in range(4 * q, 4 * q + 4):
            first[n].wait()
        for p, (start, wide, pick) in enumerate(picks):
            x = stage[4 * q * side:4 * (q + 1) * side, start:start + wide]
            x = jnp.dot(x, pick, preferred_element_type=f32).astype(bf)
            at = (2 * p + q) * 4 * side
            tile[at:at + 4 * side, :] = x[:, :128]
            tile[TILE + at:TILE + at + 4 * side, :] = x[:, 128:]
    first[8].wait()

    def phase1(i, n, buf):
        ks = list(range(2 * n, min(2 * n + 2, K)))
        w = []
        for k in ks:
            mask = only[pl.ds(pl.multiple_of(odd[k, i], 16), 16), :]
            w.append(tile[pl.ds(pl.multiple_of(src[k, i], B), B), :] * jnp.concatenate([mask] * 3, axis=0))
        if len(ks) == 2:
            none = jnp.zeros((B, 128), bf)
            lhs = jnp.concatenate([blk[i, ks[0]], blk[i, ks[1]]], axis=1)
            w = jnp.concatenate([jnp.concatenate([w[0], none], axis=1), jnp.concatenate([none, w[1]], axis=1)], axis=0)
            buf[:, n * 256:(n + 1) * 256] = jnp.dot(lhs, w, preferred_element_type=f32).astype(bf)
        else:
            buf[:, n * 256:n * 256 + 128] = jnp.dot(blk[i, ks[0]], w[0], preferred_element_type=f32).astype(bf)

    def phase2(i, n, buf):
        wide = 256 if 2 * n + 1 < K else 128
        term = jnp.dot(turned[i], buf[:, n * 256:n * 256 + wide], preferred_element_type=f32)
        for m in range(wide // 128):
            k = 2 * n + m
            acc = hi if m & 1 else lo
            acc[pl.ds(pl.multiple_of(dst[k, i], B), B), :] += term[:, m * 128:(m + 1) * 128]

    def both(i1, buf1, i2, buf2):
        for n in range(PAIRS):
            phase2(i2, n, buf2)
            phase1(i1, n, buf1)

    copy(0).wait()
    for n in range(PAIRS):
        phase1(0, n, bufa)
    def rows(p, c):
        both(2 * p + 1, bufb, 2 * p, bufa)
        @pl.when((p & 1 == 1) & (p < R // 2 - 1))
        def _():
            copy((p + 1) // 2).wait()
        both(jnp.minimum(2 * p + 2, R - 1), bufa, 2 * p + 1, bufb)
        return c
    lax.fori_loop(0, R // 2, rows, 0)

    def gathered(t2, u, each, groups):
        cols_ = []
        for n in range(each):
            rows_ = []
            for g in range(groups):
                at = (t2 + g * each + n) * B + 8 * u
                rows_.append(lo[at:at + 8, :] + hi[at:at + 8, :])
            cols_.append(jnp.concatenate(rows_, axis=0).astype(bf))
        return cols_
    def pack_rows(t, y, half, xs, place):
        step = B if half else 2 * B
        for w in range(3):
            n0, n1 = 128 * w // step, (128 * w + 127) // step + 1
            x = jnp.dot(jnp.concatenate(xs[n0:n1], axis=1), place[n0 * 128:n1 * 128, w * 128:w * 128 + 128], preferred_element_type=f32)
            for g in range(x.shape[0] // 8):
                v = x[8 * g:8 * g + 8, :]
                if t < FIRST:
                    at = (FIRST * B // 128 + t * HALF // 128 if half else t * B // 128) + g * 3 + w
                    out[y, :, at * 128:at * 128 + 128] = v.astype(bf)
                else:
                    buf2[pl.ds(y * PAD2 + (REST * B // 128 if half else 0) + g * 3 + w, 8, stride=4 * PAD2), :] = v
    away = [pltpu.make_async_copy(out.at[(here[0] + d) & 3], sends[d], osems.at[d]) for d in range(4)]
    for c in late:
        c.wait()
    for t, count in ((FIRST, REST), (0, FIRST)):
        for y, u in enumerate(FULL):
            pack_rows(t, y, False, gathered(t // 2, u, 4, count // 8), full_ref)
        for u in (1, 4):
            xs = gathered(t // 2, u, 8, count // 16)
            for y, (v, h) in enumerate(SPLIT):
                if v == u:
                    pack_rows(t, y, True, xs, half_ref.at[h])
    for c in away:
        c.start()
    for z in range(8):
        out2[z] = buf2[z * 4 * PAD2:(z + 1) * 4 * PAD2, :].astype(bf)
    for c in away:
        c.wait()

def main(src, odd, dst, here, blocks, turned, full, half, pieces):
    hbm = pl.BlockSpec(memory_space=pl.ANY)
    vmem = pl.BlockSpec(memory_space=pltpu.VMEM)
    return pl.pallas_call(
        main_kernel,
        out_shape=[jax.ShapeDtypeStruct((8, FIRST * 72), bf)] * 4 + [jax.ShapeDtypeStruct((8, 4 * PAD2, 128), bf)],
        in_specs=[pl.BlockSpec(memory_space=pltpu.SMEM)] * 4 + [hbm] * 12,
        out_specs=[hbm] * 4 + [vmem],
        scratch_shapes=[pltpu.VMEM((8 * (R // 8 * B), 8 * B), bf), pltpu.VMEM((4, 8, FIRST * 72), bf), pltpu.VMEM((8 * 4 * PAD2, 128), f32), pltpu.SemaphoreType.DMA((4,)),
                        pltpu.VMEM((R, K, B, B), bf), pltpu.VMEM((R, B, B), bf), pltpu.VMEM((2 * TILE, 128), bf)]
            + [pltpu.VMEM((T // 2 * B, 128), f32)] * 2 + [pltpu.VMEM((B, PAIRS * 256), bf)] * 2
            + [pltpu.VMEM((32, 128), bf), pltpu.VMEM((512, 384), bf), pltpu.VMEM((2, 1024, 384), bf)]
            + [pltpu.SemaphoreType.DMA((12,)), pltpu.SemaphoreType.DMA((11,))],
        compiler_params=pltpu.CompilerParams(vmem_limit_bytes=58 << 20),
        cost_estimate=pl.CostEstimate(flops=2 * 10**10, bytes_accessed=10**7, transcendentals=0),
    )(src, odd, dst, here, blocks, turned, full, half, *pieces)

def sum_y_kernel(x0, x1, x2, x3, o_ref, buf):
    def body(b, c):
        at = pl.multiple_of(b * 128, 128)
        s = (x0[:, pl.ds(at, 128)].astype(f32) + x1[:, pl.ds(at, 128)].astype(f32)) + (
            x2[:, pl.ds(at, 128)].astype(f32) + x3[:, pl.ds(at, 128)].astype(f32))
        buf[pl.ds(b, 8, stride=PAD1), :] = s
        return c
    lax.fori_loop(0, ROWS1, body, 0, unroll=21)
    for z in range(8):
        o_ref[z] = buf[z * PAD1:(z + 1) * PAD1, :].astype(bf)

def sum_y(parts):
    return pl.pallas_call(sum_y_kernel, out_shape=jax.ShapeDtypeStruct((8, PAD1, 128), bf),
                          scratch_shapes=[pltpu.VMEM((8 * PAD1, 128), f32)],
                          cost_estimate=pl.CostEstimate(flops=4 * 10**10, bytes_accessed=10**7, transcendentals=0))(*parts)

def sum_z_kernel(here, x_ref, *refs):
    outs, tot = refs[:4], refs[4]
    tot[...] = functools.reduce(lambda p, q: p + q, [x_ref[z].astype(f32) for z in range(8)])
    for d in range(4):
        outs[d][...] = tot[pl.ds(pl.multiple_of(((here[0] + d) & 3) * PAD2, 8), PAD2), :].astype(bf)

def sum_z(here, x):
    return pl.pallas_call(sum_z_kernel, out_shape=[jax.ShapeDtypeStruct((PAD2, 128), bf)] * 4,
                          in_specs=[pl.BlockSpec(memory_space=pltpu.SMEM), pl.BlockSpec(memory_space=pltpu.VMEM)],
                          scratch_shapes=[pltpu.VMEM((4 * PAD2, 128), f32)])(here, x)

def final_kernel(here, x_ref, y0, y1, y2, y3, o_ref, tot1, tot2):
    tot1[...] = functools.reduce(lambda p, q: p + q, [x_ref[z].astype(f32) for z in range(8)])
    tot2[...] = functools.reduce(lambda p, q: p + q, [y[...].astype(f32) for y in (y0, y1, y2, y3)])
    odd = here[0] & 1
    l0 = lax.broadcasted_iota(jnp.int32, (384, 128), 0)
    l1 = lax.broadcasted_iota(jnp.int32, (384, 128), 1)
    for tot, total, slot in ((tot1, FIRST, 0), (tot2, REST, FIRST // CR)):
        acc = jnp.zeros((total, 128), f32)
        for step, start, place in ((B, 0, odd * HALF), (HALF, total * B // 128, (1 - odd) * B)):
            side = 384 // step
            groups = total // side
            pick = (l0 % step + place == l1).astype(f32).astype(bf)
            lane = lax.broadcasted_iota(jnp.int32, (1, side, 128), 2)
            which = lax.broadcasted_iota(jnp.int32, (1, side, 128), 1)
            xs = [tot[pl.ds(start + w, groups, stride=3), :] for w in range(3)]
            for _ in range(3):
                wide = []
                for w in range(3):
                    top = xs[w].astype(bf).astype(f32)
                    xs[w] = xs[w] - top
                    mine = (lane + w * 128) // step == which
                    wide.append(jnp.where(mine, top[:, None, :], 0.0).reshape(total, 128).astype(bf))
                acc = acc + jnp.dot(jnp.concatenate(wide, axis=1), pick, preferred_element_type=f32)
        o_ref[slot:slot + total // CR] = acc[:, :72].reshape(total // CR, CR, 72)

def final(here, x, parts):
    return pl.pallas_call(final_kernel, out_shape=jax.ShapeDtypeStruct((KC, CR, 72), f32),
                          in_specs=[pl.BlockSpec(memory_space=pltpu.SMEM)] + [pl.BlockSpec(memory_space=pltpu.VMEM)] * 5,
                          scratch_shapes=[pltpu.VMEM((PAD1, 128), f32), pltpu.VMEM((PAD2, 128), f32)])(here, x, *parts)

ZG = [[z * 4 + y for z in range(8)] for y in range(4)]

def along_x(x, by):
    return lax.ppermute(x, "row", [(i, (i + 2 * by) % 8) for i in range(8)])

def across(x):
    return lax.ppermute(x, "row", [(i, i ^ 1) for i in range(8)])

def along_y(x, by):
    return lax.ppermute(x, "col", [(4 * z + y, 4 * z + (y + by) % 4) for z in range(8) for y in range(4)])

def exchange_z(x):
    return lax.all_to_all(x, "col", 0, 0, axis_index_groups=ZG, tiled=True)

def indices(columns, aggregate, slots):
    row = lax.axis_index("row")
    owner = columns // R
    apart = ((owner >> 1) - (row >> 1)) & 3
    piece = jnp.where(apart == 3, 2, jnp.where(apart == 2, 3, apart)) + 4 * ((owner ^ row) & 1)
    t = columns % R
    at = ((t & 7) >> 1) * R + piece * (R // 8) + (t >> 3)
    target = slots * CR + aggregate[:, None]
    odd = target & 1
    return (at * B + ((t ^ odd) & 1) * TILE).T, (odd * 16).T, ((target >> 1) * B).T

def shards(blocks, prolong, columns, aggregate, slots):
    packed = pack(prolong)
    mine = [packed, along_x(packed, -1), along_x(packed, 1), along_x(packed, 2)]
    index = indices(columns, aggregate, slots)
    turned = turn(prolong)
    near, turned, index = lax.optimization_barrier((mine, turned, index))
    pieces = near + [across(x) for x in near]
    here = (lax.axis_index("col") & 3).reshape(1)
    *sends, other = main(*index, here, blocks, *turned, pieces)
    parts = [sends[0]] + [along_y(sends[d], d) for d in range(1, 4)]
    other = sum_z(here, exchange_z(other))
    first = exchange_z(sum_y(parts))
    other = [other[0]] + [along_y(other[d], d) for d in range(1, 4)]
    return final(here, first, other).transpose(1, 0, 2)


def solution(mesh):
    return jax.shard_map(
        shards,
        mesh=mesh,
        in_specs=(
            jax.sharding.PartitionSpec(("row", "col"), None, None, None),
            jax.sharding.PartitionSpec(("row", "col"), None, None),
            jax.sharding.PartitionSpec(("row", "col"), None),
            jax.sharding.PartitionSpec(("row", "col")),
            jax.sharding.PartitionSpec(("row", "col"), None),
        ),
        out_specs=jax.sharding.PartitionSpec("row", None, "col"),
        check_vma=False,
    )
```

```python
import functools
import jax, jax.numpy as jnp
from jax import lax
from jax.experimental import pallas as pl
from jax.experimental.pallas import tpu as pltpu
bf, f32 = jnp.bfloat16, jnp.float32
B, K, KC, CR, R = 48, 27, 27, 16, 48
PAIRS = (K + 1) // 2
PIECE = R // 2 * B
HALF = B // 2
TILE = 8 * PIECE
FULL = (0, 2, 3, 5)
SPLIT = ((1, 0), (1, 1), (4, 0), (4, 1))

T = KC * CR
FIRST = 336
REST = T - FIRST
ROWS1 = FIRST * 72 // 128
PAD1 = 192
ROWS2 = REST * 72 // 128
PAD2 = 56

def pack_kernel(p_ref, o_ref):
    for g in range(R // 8):
        o_ref[g * B:(g + 1) * B, :] = jnp.concatenate([p_ref[8 * g + m] for m in range(8)], axis=1)

def pack(p):
    return pl.pallas_call(pack_kernel, out_shape=jax.ShapeDtypeStruct((R // 8 * B, 8 * B), bf))(p)

def placing(n, step, off):
    row = lax.broadcasted_iota(jnp.int32, (n * 128, 384), 0)
    col = lax.broadcasted_iota(jnp.int32, (n * 128, 384), 1)
    t, c = col // step, col % step
    return (row == (t // 2) * 128 + (t % 2) * B + off + c).astype(f32).astype(bf)

def turn_kernel(p_ref, o_ref, full_ref, half_ref):
    row = lax.broadcasted_iota(jnp.int32, (B, B), 0)
    a = lax.broadcasted_iota(jnp.int32, (B, B), 1)
    pick = (row == (a % 6) * 8 + a // 6).astype(f32).astype(bf)
    for i in range(R):
        o_ref[i] = lax.dot_general(pick, p_ref[i], (((1,), (1,)), ((), ())), preferred_element_type=f32).astype(bf)
    full_ref[...] = placing(4, B, 0)
    for h in range(2):
        half_ref[h] = placing(8, HALF, h * HALF)

def turn(p):
    return pl.pallas_call(turn_kernel, out_shape=[jax.ShapeDtypeStruct((R, B, B), bf), jax.ShapeDtypeStruct((512, 384), bf),
                                                  jax.ShapeDtypeStruct((2, 1024, 384), bf)],
                          cost_estimate=pl.CostEstimate(flops=10**7, bytes_accessed=2 * 10**6, transcendentals=0))(p)

def main_kernel(src, odd, dst, here, blk_hbm, turned_hbm, full_hbm, half_hbm, *rest):
    pieces, sends, out2, (stage, out, buf2, osems, blk, turned, tile, lo, hi, bufa, bufb, only, full_ref, half_ref, sems, psems) = (
        rest[:8], rest[8:12], rest[12], rest[13:])
    first = [pltpu.make_async_copy(piece, stage.at[pl.ds(n * (R // 8 * B), R // 8 * B)], psems.at[n]) for n, piece in enumerate(pieces)]
    first.append(pltpu.make_async_copy(turned_hbm, turned, psems.at[8]))
    CH = 4
    def copy(n):
        return pltpu.make_async_copy(blk_hbm.at[pl.ds(n * CH, CH)], blk.at[pl.ds(n * CH, CH)], sems.at[n])
    late = [pltpu.make_async_copy(full_hbm, full_ref, psems.at[9]), pltpu.make_async_copy(half_hbm, half_ref, psems.at[10])]
    for c in first:
        c.start()
    for n in range(2):
        copy(n).start()

    def zero(n, c):
        z = pl.multiple_of(n * 384, 8)
        lo[pl.ds(z, 384), :] = jnp.zeros((384, 128), f32)
        hi[pl.ds(z, 384), :] = jnp.zeros((384, 128), f32)
        return c
    lax.fori_loop(0, T // 2 * B // 384, zero, 0)
    lane = lax.broadcasted_iota(jnp.int32, (32, 128), 1)
    row = lax.broadcasted_iota(jnp.int32, (32, 128), 0)
    only[...] = ((lane >= B * (row // 16)) & (lane < B * (row // 16) + B)).astype(f32).astype(bf)

    picks = []
    for p in range(4):
        start = 2 * B * p // 128 * 128
        wide = min(256, 8 * B - start)
        l0 = lax.broadcasted_iota(jnp.int32, (wide, 256), 0) + start - 2 * B * p
        l1 = lax.broadcasted_iota(jnp.int32, (wide, 256), 1)
        other = l1 - 128
        keep = (l1 < 2 * B) & (l0 == l1)
        change = (other >= 0) & (other < 2 * B) & (l0 == jnp.where(other < B, other + B, other - B))
        picks.append((start, wide, (keep | change).astype(f32).astype(bf)))
    side = R // 8 * B
    for q in range(2):
        for n in range(4 * q, 4 * q + 4):
            first[n].wait()
        if q == 1:
            for n in range(2, R // CH):
                copy(n).start()
            for c in late:
                c.start()
        for p, (start, wide, pick) in enumerate(picks):
            x = stage[4 * q * side:4 * (q + 1) * side, start:start + wide]
            x = jnp.dot(x, pick, preferred_element_type=f32).astype(bf)
            at = (2 * p + q) * 4 * side
            tile[at:at + 4 * side, :] = x[:, :128]
            tile[TILE + at:TILE + at + 4 * side, :] = x[:, 128:]
    first[8].wait()

    def phase1(i, n, buf):
        ks = list(range(2 * n, min(2 * n + 2, K)))
        w = []
        for k in ks:
            mask = only[pl.ds(pl.multiple_of(odd[k, i], 16), 16), :]
            w.append(tile[pl.ds(pl.multiple_of(src[k, i], B), B), :] * jnp.concatenate([mask] * 3, axis=0))
        if len(ks) == 2:
            none = jnp.zeros((B, 128), bf)
            lhs = jnp.concatenate([blk[i, ks[0]], blk[i, ks[1]]], axis=1)
            w = jnp.concatenate([jnp.concatenate([w[0], none], axis=1), jnp.concatenate([none, w[1]], axis=1)], axis=0)
            buf[:, n * 256:(n + 1) * 256] = jnp.dot(lhs, w, preferred_element_type=f32).astype(bf)
        else:
            buf[:, n * 256:n * 256 + 128] = jnp.dot(blk[i, ks[0]], w[0], preferred_element_type=f32).astype(bf)

    def phase2(i, n, buf):
        wide = 256 if 2 * n + 1 < K else 128
        term = jnp.dot(turned[i], buf[:, n * 256:n * 256 + wide], preferred_element_type=f32)
        for m in range(wide // 128):
            k = 2 * n + m
            acc = hi if m & 1 else lo
            acc[pl.ds(pl.multiple_of(dst[k, i], B), B), :] += term[:, m * 128:(m + 1) * 128]

    def both(i1, buf1, i2, buf2):
        for n in range(PAIRS):
            phase2(i2, n, buf2)
            phase1(i1, n, buf1)

    copy(0).wait()
    for n in range(PAIRS):
        phase1(0, n, bufa)
    def rows(p, c):
        both(2 * p + 1, bufb, 2 * p, bufa)
        @pl.when((p & 1 == 1) & (p < R // 2 - 1))
        def _():
            copy((p + 1) // 2).wait()
        both(jnp.minimum(2 * p + 2, R - 1), bufa, 2 * p + 1, bufb)
        return c
    lax.fori_loop(0, R // 2, rows, 0)

    def gathered(t2, u, each, groups):
        cols_ = []
        for n in range(each):
            rows_ = []
            for g in range(groups):
                at = (t2 + g * each + n) * B + 8 * u
                rows_.append(lo[at:at + 8, :] + hi[at:at + 8, :])
            cols_.append(jnp.concatenate(rows_, axis=0).astype(bf))
        return cols_
    def pack_rows(t, y, half, xs, place):
        step = B if half else 2 * B
        for w in range(3):
            n0, n1 = 128 * w // step, (128 * w + 127) // step + 1
            x = jnp.dot(jnp.concatenate(xs[n0:n1], axis=1), place[n0 * 128:n1 * 128, w * 128:w * 128 + 128], preferred_element_type=f32)
            for g in range(x.shape[0] // 8):
                v = x[8 * g:8 * g + 8, :]
                if t < FIRST:
                    at = (FIRST * B // 128 + t * HALF // 128 if half else t * B // 128) + g * 3 + w
                    out[y, :, at * 128:at * 128 + 128] = v.astype(bf)
                else:
                    buf2[pl.ds(y * PAD2 + (REST * B // 128 if half else 0) + g * 3 + w, 8, stride=4 * PAD2), :] = v
    away = [pltpu.make_async_copy(out.at[(here[0] + d) & 3], sends[d], osems.at[d]) for d in range(4)]
    for c in late:
        c.wait()
    for t, count in ((FIRST, REST), (0, FIRST)):
        for y, u in enumerate(FULL):
            pack_rows(t, y, False, gathered(t // 2, u, 4, count // 8), full_ref)
        for u in (1, 4):
            xs = gathered(t // 2, u, 8, count // 16)
            for y, (v, h) in enumerate(SPLIT):
                if v == u:
                    pack_rows(t, y, True, xs, half_ref.at[h])
    for c in away:
        c.start()
    for z in range(8):
        out2[z] = buf2[z * 4 * PAD2:(z + 1) * 4 * PAD2, :].astype(bf)
    for c in away:
        c.wait()

def main(src, odd, dst, here, blocks, turned, full, half, pieces):
    hbm = pl.BlockSpec(memory_space=pl.ANY)
    vmem = pl.BlockSpec(memory_space=pltpu.VMEM)
    return pl.pallas_call(
        main_kernel,
        out_shape=[jax.ShapeDtypeStruct((8, FIRST * 72), bf)] * 4 + [jax.ShapeDtypeStruct((8, 4 * PAD2, 128), bf)],
        in_specs=[pl.BlockSpec(memory_space=pltpu.SMEM)] * 4 + [hbm] * 12,
        out_specs=[hbm] * 4 + [vmem],
        scratch_shapes=[pltpu.VMEM((8 * (R // 8 * B), 8 * B), bf), pltpu.VMEM((4, 8, FIRST * 72), bf), pltpu.VMEM((8 * 4 * PAD2, 128), f32), pltpu.SemaphoreType.DMA((4,)),
                        pltpu.VMEM((R, K, B, B), bf), pltpu.VMEM((R, B, B), bf), pltpu.VMEM((2 * TILE, 128), bf)]
            + [pltpu.VMEM((T // 2 * B, 128), f32)] * 2 + [pltpu.VMEM((B, PAIRS * 256), bf)] * 2
            + [pltpu.VMEM((32, 128), bf), pltpu.VMEM((512, 384), bf), pltpu.VMEM((2, 1024, 384), bf)]
            + [pltpu.SemaphoreType.DMA((12,)), pltpu.SemaphoreType.DMA((11,))],
        compiler_params=pltpu.CompilerParams(vmem_limit_bytes=58 << 20),
        cost_estimate=pl.CostEstimate(flops=2 * 10**10, bytes_accessed=10**7, transcendentals=0),
    )(src, odd, dst, here, blocks, turned, full, half, *pieces)

def sum_y_kernel(x0, x1, x2, x3, o_ref, buf):
    def body(b, c):
        at = pl.multiple_of(b * 128, 128)
        s = (x0[:, pl.ds(at, 128)].astype(f32) + x1[:, pl.ds(at, 128)].astype(f32)) + (
            x2[:, pl.ds(at, 128)].astype(f32) + x3[:, pl.ds(at, 128)].astype(f32))
        buf[pl.ds(b, 8, stride=PAD1), :] = s
        return c
    lax.fori_loop(0, ROWS1, body, 0, unroll=21)
    for z in range(8):
        o_ref[z] = buf[z * PAD1:(z + 1) * PAD1, :].astype(bf)

def sum_y(parts):
    return pl.pallas_call(sum_y_kernel, out_shape=jax.ShapeDtypeStruct((8, PAD1, 128), bf),
                          scratch_shapes=[pltpu.VMEM((8 * PAD1, 128), f32)],
                          cost_estimate=pl.CostEstimate(flops=4 * 10**10, bytes_accessed=10**7, transcendentals=0))(*parts)

def sum_z_kernel(here, x_ref, *refs):
    outs, tot = refs[:4], refs[4]
    tot[...] = functools.reduce(lambda p, q: p + q, [x_ref[z].astype(f32) for z in range(8)])
    for d in range(4):
        outs[d][...] = tot[pl.ds(pl.multiple_of(((here[0] + d) & 3) * PAD2, 8), PAD2), :].astype(bf)

def sum_z(here, x):
    return pl.pallas_call(sum_z_kernel, out_shape=[jax.ShapeDtypeStruct((PAD2, 128), bf)] * 4,
                          in_specs=[pl.BlockSpec(memory_space=pltpu.SMEM), pl.BlockSpec(memory_space=pltpu.VMEM)],
                          scratch_shapes=[pltpu.VMEM((4 * PAD2, 128), f32)])(here, x)

def final_kernel(here, x_ref, y0, y1, y2, y3, o_ref, tot1, tot2):
    tot1[...] = functools.reduce(lambda p, q: p + q, [x_ref[z].astype(f32) for z in range(8)])
    tot2[...] = functools.reduce(lambda p, q: p + q, [y[...].astype(f32) for y in (y0, y1, y2, y3)])
    odd = here[0] & 1
    l0 = lax.broadcasted_iota(jnp.int32, (384, 128), 0)
    l1 = lax.broadcasted_iota(jnp.int32, (384, 128), 1)
    for tot, total, slot in ((tot1, FIRST, 0), (tot2, REST, FIRST // CR)):
        acc = jnp.zeros((total, 128), f32)
        for step, start, place in ((B, 0, odd * HALF), (HALF, total * B // 128, (1 - odd) * B)):
            side = 384 // step
            groups = total // side
            pick = (l0 % step + place == l1).astype(f32).astype(bf)
            lane = lax.broadcasted_iota(jnp.int32, (1, side, 128), 2)
            which = lax.broadcasted_iota(jnp.int32, (1, side, 128), 1)
            xs = [tot[pl.ds(start + w, groups, stride=3), :] for w in range(3)]
            for _ in range(3):
                wide = []
                for w in range(3):
                    top = xs[w].astype(bf).astype(f32)
                    xs[w] = xs[w] - top
                    mine = (lane + w * 128) // step == which
                    wide.append(jnp.where(mine, top[:, None, :], 0.0).reshape(total, 128).astype(bf))
                acc = acc + jnp.dot(jnp.concatenate(wide, axis=1), pick, preferred_element_type=f32)
        o_ref[slot:slot + total // CR] = acc[:, :72].reshape(total // CR, CR, 72)

def final(here, x, parts):
    return pl.pallas_call(final_kernel, out_shape=jax.ShapeDtypeStruct((KC, CR, 72), f32),
                          in_specs=[pl.BlockSpec(memory_space=pltpu.SMEM)] + [pl.BlockSpec(memory_space=pltpu.VMEM)] * 5,
                          scratch_shapes=[pltpu.VMEM((PAD1, 128), f32), pltpu.VMEM((PAD2, 128), f32)])(here, x, *parts)

ZG = [[z * 4 + y for z in range(8)] for y in range(4)]

def along_x(x, by):
    return lax.ppermute(x, "row", [(i, (i + 2 * by) % 8) for i in range(8)])

def across(x):
    return lax.ppermute(x, "row", [(i, i ^ 1) for i in range(8)])

def along_y(x, by):
    return lax.ppermute(x, "col", [(4 * z + y, 4 * z + (y + by) % 4) for z in range(8) for y in range(4)])

def exchange_z(x):
    return lax.all_to_all(x, "col", 0, 0, axis_index_groups=ZG, tiled=True)

def indices(columns, aggregate, slots):
    row = lax.axis_index("row")
    owner = columns // R
    apart = ((owner >> 1) - (row >> 1)) & 3
    piece = jnp.where(apart == 3, 2, jnp.where(apart == 2, 3, apart)) + 4 * ((owner ^ row) & 1)
    t = columns % R
    at = ((t & 7) >> 1) * R + piece * (R // 8) + (t >> 3)
    target = slots * CR + aggregate[:, None]
    odd = target & 1
    return (at * B + ((t ^ odd) & 1) * TILE).T, (odd * 16).T, ((target >> 1) * B).T

def shards(blocks, prolong, columns, aggregate, slots):
    packed = pack(prolong)
    mine = [packed, along_x(packed, -1), along_x(packed, 1), along_x(packed, 2)]
    index = indices(columns, aggregate, slots)
    turned = turn(prolong)
    near, turned, index = lax.optimization_barrier((mine, turned, index))
    pieces = near + [across(x) for x in near]
    here = (lax.axis_index("col") & 3).reshape(1)
    *sends, other = main(*index, here, blocks, *turned, pieces)
    parts = [sends[0]] + [along_y(sends[d], d) for d in range(1, 4)]
    other = sum_z(here, exchange_z(other))
    first = exchange_z(sum_y(parts))
    other = [other[0]] + [along_y(other[d], d) for d in range(1, 4)]
    return final(here, first, other).transpose(1, 0, 2)


def solution(mesh):
    return jax.shard_map(
        shards,
        mesh=mesh,
        in_specs=(
            jax.sharding.PartitionSpec(("row", "col"), None, None, None),
            jax.sharding.PartitionSpec(("row", "col"), None, None),
            jax.sharding.PartitionSpec(("row", "col"), None),
            jax.sharding.PartitionSpec(("row", "col")),
            jax.sharding.PartitionSpec(("row", "col"), None),
        ),
        out_specs=jax.sharding.PartitionSpec("row", None, "col"),
        check_vma=False,
    )
```

```python
import functools
import jax, jax.numpy as jnp
from jax import lax
from jax.experimental import pallas as pl
from jax.experimental.pallas import tpu as pltpu
bf, f32 = jnp.bfloat16, jnp.float32
B, K, KC, CR, R = 48, 27, 27, 16, 48
PAIRS = (K + 1) // 2
PIECE = R // 2 * B
HALF = B // 2
TILE = 8 * PIECE
FULL = (0, 2, 3, 5)
SPLIT = ((1, 0), (1, 1), (4, 0), (4, 1))

T = KC * CR
FIRST = 336
REST = T - FIRST
ROWS1 = FIRST * 72 // 128
PAD1 = 192
ROWS2 = REST * 72 // 128
PAD2 = 56

def pack_kernel(p_ref, o_ref):
    for g in range(R // 8):
        o_ref[g * B:(g + 1) * B, :] = jnp.concatenate([p_ref[8 * g + m] for m in range(8)], axis=1)

def pack(p):
    return pl.pallas_call(pack_kernel, out_shape=jax.ShapeDtypeStruct((R // 8 * B, 8 * B), bf))(p)

def placing(n, step, off):
    row = lax.broadcasted_iota(jnp.int32, (n * 128, 384), 0)
    col = lax.broadcasted_iota(jnp.int32, (n * 128, 384), 1)
    t, c = col // step, col % step
    return (row == (t // 2) * 128 + (t % 2) * B + off + c).astype(f32).astype(bf)

def turn_kernel(p_ref, o_ref, full_ref, half_ref):
    row = lax.broadcasted_iota(jnp.int32, (B, B), 0)
    a = lax.broadcasted_iota(jnp.int32, (B, B), 1)
    pick = (row == (a % 6) * 8 + a // 6).astype(f32).astype(bf)
    for i in range(R):
        o_ref[i] = lax.dot_general(pick, p_ref[i], (((1,), (1,)), ((), ())), preferred_element_type=f32).astype(bf)
    full_ref[...] = placing(4, B, 0)
    for h in range(2):
        half_ref[h] = placing(8, HALF, h * HALF)

def turn(p):
    return pl.pallas_call(turn_kernel, out_shape=[jax.ShapeDtypeStruct((R, B, B), bf), jax.ShapeDtypeStruct((512, 384), bf),
                                                  jax.ShapeDtypeStruct((2, 1024, 384), bf)],
                          cost_estimate=pl.CostEstimate(flops=10**7, bytes_accessed=2 * 10**6, transcendentals=0))(p)

def main_kernel(src, odd, dst, here, blk_hbm, turned_hbm, full_hbm, half_hbm, *rest):
    pieces, sends, out2, (stage, out, buf2, osems, blk, turned, tile, lo, hi, bufa, bufb, only, full_ref, half_ref, sems, psems) = (
        rest[:8], rest[8:12], rest[12], rest[13:])
    first = [pltpu.make_async_copy(piece, stage.at[pl.ds(n * (R // 8 * B), R // 8 * B)], psems.at[n]) for n, piece in enumerate(pieces)]
    first.append(pltpu.make_async_copy(turned_hbm, turned, psems.at[8]))
    CH = 4
    def copy(n):
        return pltpu.make_async_copy(blk_hbm.at[pl.ds(n * CH, CH)], blk.at[pl.ds(n * CH, CH)], sems.at[n])
    late = [pltpu.make_async_copy(full_hbm, full_ref, psems.at[9]), pltpu.make_async_copy(half_hbm, half_ref, psems.at[10])]
    for c in first:
        c.start()
    copy(0).start()

    def zero(n, c):
        z = pl.multiple_of(n * 384, 8)
        lo[pl.ds(z, 384), :] = jnp.zeros((384, 128), f32)
        hi[pl.ds(z, 384), :] = jnp.zeros((384, 128), f32)
        return c
    lax.fori_loop(0, T // 2 * B // 384, zero, 0)
    lane = lax.broadcasted_iota(jnp.int32, (32, 128), 1)
    row = lax.broadcasted_iota(jnp.int32, (32, 128), 0)
    only[...] = ((lane >= B * (row // 16)) & (lane < B * (row // 16) + B)).astype(f32).astype(bf)

    picks = []
    for p in range(4):
        start = 2 * B * p // 128 * 128
        wide = min(256, 8 * B - start)
        l0 = lax.broadcasted_iota(jnp.int32, (wide, 256), 0) + start - 2 * B * p
        l1 = lax.broadcasted_iota(jnp.int32, (wide, 256), 1)
        other = l1 - 128
        keep = (l1 < 2 * B) & (l0 == l1)
        change = (other >= 0) & (other < 2 * B) & (l0 == jnp.where(other < B, other + B, other - B))
        picks.append((start, wide, (keep | change).astype(f32).astype(bf)))
    side = R // 8 * B
    for q in range(2):
        for n in range(4 * q, 4 * q + 4):
            first[n].wait()
        if q == 1:
            for n in range(1, R // CH):
                copy(n).start()
            for c in late:
                c.start()
        for p, (start, wide, pick) in enumerate(picks):
            x = stage[4 * q * side:4 * (q + 1) * side, start:start + wide]
            x = jnp.dot(x, pick, preferred_element_type=f32).astype(bf)
            at = (2 * p + q) * 4 * side
            tile[at:at + 4 * side, :] = x[:, :128]
            tile[TILE + at:TILE + at + 4 * side, :] = x[:, 128:]
    first[8].wait()

    def phase1(i, n, buf):
        ks = list(range(2 * n, min(2 * n + 2, K)))
        w = []
        for k in ks:
            mask = only[pl.ds(pl.multiple_of(odd[k, i], 16), 16), :]
            w.append(tile[pl.ds(pl.multiple_of(src[k, i], B), B), :] * jnp.concatenate([mask] * 3, axis=0))
        if len(ks) == 2:
            none = jnp.zeros((B, 128), bf)
            lhs = jnp.concatenate([blk[i, ks[0]], blk[i, ks[1]]], axis=1)
            w = jnp.concatenate([jnp.concatenate([w[0], none], axis=1), jnp.concatenate([none, w[1]], axis=1)], axis=0)
            buf[:, n * 256:(n + 1) * 256] = jnp.dot(lhs, w, preferred_element_type=f32).astype(bf)
        else:
            buf[:, n * 256:n * 256 + 128] = jnp.dot(blk[i, ks[0]], w[0], preferred_element_type=f32).astype(bf)

    def phase2(i, n, buf):
        wide = min(4, K - 2 * n) * 128
        term = jnp.dot(turned[i], buf[:, n * 256:n * 256 + wide], preferred_element_type=f32)
        for m in range(wide // 128):
            k = 2 * n + m
            acc = hi if m & 1 else lo
            acc[pl.ds(pl.multiple_of(dst[k, i], B), B), :] += term[:, m * 128:(m + 1) * 128]

    def both(i1, buf1, i2, buf2):
        for n in range(0, PAIRS, 2):
            phase2(i2, n, buf2)
            phase1(i1, n, buf1)
            phase1(i1, n + 1, buf1)

    copy(0).wait()
    for n in range(PAIRS):
        phase1(0, n, bufa)
    def rows(p, c):
        both(2 * p + 1, bufb, 2 * p, bufa)
        @pl.when((p & 1 == 1) & (p < R // 2 - 1))
        def _():
            copy((p + 1) // 2).wait()
        both(jnp.minimum(2 * p + 2, R - 1), bufa, 2 * p + 1, bufb)
        return c
    lax.fori_loop(0, R // 2, rows, 0)

    def gathered(t2, u, each, groups):
        cols_ = []
        for n in range(each):
            rows_ = []
            for g in range(groups):
                at = (t2 + g * each + n) * B + 8 * u
                rows_.append(lo[at:at + 8, :] + hi[at:at + 8, :])
            cols_.append(jnp.concatenate(rows_, axis=0).astype(bf))
        return cols_
    def pack_rows(t, y, half, xs, place):
        step = B if half else 2 * B
        for w in range(3):
            n0, n1 = 128 * w // step, (128 * w + 127) // step + 1
            x = jnp.dot(jnp.concatenate(xs[n0:n1], axis=1), place[n0 * 128:n1 * 128, w * 128:w * 128 + 128], preferred_element_type=f32)
            for g in range(x.shape[0] // 8):
                v = x[8 * g:8 * g + 8, :]
                if t < FIRST:
                    at = (FIRST * B // 128 + t * HALF // 128 if half else t * B // 128) + g * 3 + w
                    out[y, :, at * 128:at * 128 + 128] = v.astype(bf)
                else:
                    buf2[pl.ds(y * PAD2 + (REST * B // 128 if half else 0) + g * 3 + w, 8, stride=4 * PAD2), :] = v
    away = [pltpu.make_async_copy(out.at[(here[0] + d) & 3], sends[d], osems.at[d]) for d in range(4)]
    for c in late:
        c.wait()
    for t, count in ((FIRST, REST), (0, FIRST)):
        for y, u in enumerate(FULL):
            pack_rows(t, y, False, gathered(t // 2, u, 4, count // 8), full_ref)
        for u in (1, 4):
            xs = gathered(t // 2, u, 8, count // 16)
            for y, (v, h) in enumerate(SPLIT):
                if v == u:
                    pack_rows(t, y, True, xs, half_ref.at[h])
    for c in away:
        c.start()
    for z in range(8):
        out2[z] = buf2[z * 4 * PAD2:(z + 1) * 4 * PAD2, :].astype(bf)
    for c in away:
        c.wait()

def main(src, odd, dst, here, blocks, turned, full, half, pieces):
    hbm = pl.BlockSpec(memory_space=pl.ANY)
    vmem = pl.BlockSpec(memory_space=pltpu.VMEM)
    return pl.pallas_call(
        main_kernel,
        out_shape=[jax.ShapeDtypeStruct((8, FIRST * 72), bf)] * 4 + [jax.ShapeDtypeStruct((8, 4 * PAD2, 128), bf)],
        in_specs=[pl.BlockSpec(memory_space=pltpu.SMEM)] * 4 + [hbm] * 12,
        out_specs=[hbm] * 4 + [vmem],
        scratch_shapes=[pltpu.VMEM((8 * (R // 8 * B), 8 * B), bf), pltpu.VMEM((4, 8, FIRST * 72), bf), pltpu.VMEM((8 * 4 * PAD2, 128), f32), pltpu.SemaphoreType.DMA((4,)),
                        pltpu.VMEM((R, K, B, B), bf), pltpu.VMEM((R, B, B), bf), pltpu.VMEM((2 * TILE, 128), bf)]
            + [pltpu.VMEM((T // 2 * B, 128), f32)] * 2 + [pltpu.VMEM((B, PAIRS * 256), bf)] * 2
            + [pltpu.VMEM((32, 128), bf), pltpu.VMEM((512, 384), bf), pltpu.VMEM((2, 1024, 384), bf)]
            + [pltpu.SemaphoreType.DMA((12,)), pltpu.SemaphoreType.DMA((11,))],
        compiler_params=pltpu.CompilerParams(vmem_limit_bytes=58 << 20),
        cost_estimate=pl.CostEstimate(flops=2 * 10**10, bytes_accessed=10**7, transcendentals=0),
    )(src, odd, dst, here, blocks, turned, full, half, *pieces)

def sum_y_kernel(x0, x1, x2, x3, o_ref, buf):
    def body(b, c):
        at = pl.multiple_of(b * 128, 128)
        s = (x0[:, pl.ds(at, 128)].astype(f32) + x1[:, pl.ds(at, 128)].astype(f32)) + (
            x2[:, pl.ds(at, 128)].astype(f32) + x3[:, pl.ds(at, 128)].astype(f32))
        buf[pl.ds(b, 8, stride=PAD1), :] = s
        return c
    lax.fori_loop(0, ROWS1, body, 0, unroll=21)
    for z in range(8):
        o_ref[z] = buf[z * PAD1:(z + 1) * PAD1, :].astype(bf)

def sum_y(parts):
    return pl.pallas_call(sum_y_kernel, out_shape=jax.ShapeDtypeStruct((8, PAD1, 128), bf),
                          scratch_shapes=[pltpu.VMEM((8 * PAD1, 128), f32)],
                          cost_estimate=pl.CostEstimate(flops=4 * 10**10, bytes_accessed=10**7, transcendentals=0))(*parts)

def sum_z_kernel(here, x_ref, *refs):
    outs, tot = refs[:4], refs[4]
    tot[...] = functools.reduce(lambda p, q: p + q, [x_ref[z].astype(f32) for z in range(8)])
    for d in range(4):
        outs[d][...] = tot[pl.ds(pl.multiple_of(((here[0] + d) & 3) * PAD2, 8), PAD2), :].astype(bf)

def sum_z(here, x):
    return pl.pallas_call(sum_z_kernel, out_shape=[jax.ShapeDtypeStruct((PAD2, 128), bf)] * 4,
                          in_specs=[pl.BlockSpec(memory_space=pltpu.SMEM), pl.BlockSpec(memory_space=pltpu.VMEM)],
                          scratch_shapes=[pltpu.VMEM((4 * PAD2, 128), f32)])(here, x)

def final_kernel(here, x_ref, y0, y1, y2, y3, o_ref, tot1, tot2):
    tot1[...] = functools.reduce(lambda p, q: p + q, [x_ref[z].astype(f32) for z in range(8)])
    tot2[...] = functools.reduce(lambda p, q: p + q, [y[...].astype(f32) for y in (y0, y1, y2, y3)])
    odd = here[0] & 1
    l0 = lax.broadcasted_iota(jnp.int32, (384, 128), 0)
    l1 = lax.broadcasted_iota(jnp.int32, (384, 128), 1)
    for tot, total, slot in ((tot1, FIRST, 0), (tot2, REST, FIRST // CR)):
        acc = jnp.zeros((total, 128), f32)
        for step, start, place in ((B, 0, odd * HALF), (HALF, total * B // 128, (1 - odd) * B)):
            side = 384 // step
            groups = total // side
            pick = (l0 % step + place == l1).astype(f32).astype(bf)
            lane = lax.broadcasted_iota(jnp.int32, (1, side, 128), 2)
            which = lax.broadcasted_iota(jnp.int32, (1, side, 128), 1)
            xs = [tot[pl.ds(start + w, groups, stride=3), :] for w in range(3)]
            for _ in range(3):
                wide = []
                for w in range(3):
                    top = xs[w].astype(bf).astype(f32)
                    xs[w] = xs[w] - top
                    mine = (lane + w * 128) // step == which
                    wide.append(jnp.where(mine, top[:, None, :], 0.0).reshape(total, 128).astype(bf))
                acc = acc + jnp.dot(jnp.concatenate(wide, axis=1), pick, preferred_element_type=f32)
        o_ref[slot:slot + total // CR] = acc[:, :72].reshape(total // CR, CR, 72)

def final(here, x, parts):
    return pl.pallas_call(final_kernel, out_shape=jax.ShapeDtypeStruct((KC, CR, 72), f32),
                          in_specs=[pl.BlockSpec(memory_space=pltpu.SMEM)] + [pl.BlockSpec(memory_space=pltpu.VMEM)] * 5,
                          scratch_shapes=[pltpu.VMEM((PAD1, 128), f32), pltpu.VMEM((PAD2, 128), f32)])(here, x, *parts)

ZG = [[z * 4 + y for z in range(8)] for y in range(4)]

def along_x(x, by):
    return lax.ppermute(x, "row", [(i, (i + 2 * by) % 8) for i in range(8)])

def across(x):
    return lax.ppermute(x, "row", [(i, i ^ 1) for i in range(8)])

def along_y(x, by):
    return lax.ppermute(x, "col", [(4 * z + y, 4 * z + (y + by) % 4) for z in range(8) for y in range(4)])

def exchange_z(x):
    return lax.all_to_all(x, "col", 0, 0, axis_index_groups=ZG, tiled=True)

def indices(columns, aggregate, slots):
    row = lax.axis_index("row")
    owner = columns // R
    apart = ((owner >> 1) - (row >> 1)) & 3
    piece = jnp.where(apart == 3, 2, jnp.where(apart == 2, 3, apart)) + 4 * ((owner ^ row) & 1)
    t = columns % R
    at = ((t & 7) >> 1) * R + piece * (R // 8) + (t >> 3)
    target = slots * CR + aggregate[:, None]
    odd = target & 1
    return (at * B + ((t ^ odd) & 1) * TILE).T, (odd * 16).T, ((target >> 1) * B).T

def shards(blocks, prolong, columns, aggregate, slots):
    packed = pack(prolong)
    mine = [packed, along_x(packed, -1), along_x(packed, 1), along_x(packed, 2)]
    index = indices(columns, aggregate, slots)
    turned = turn(prolong)
    near, turned, index = lax.optimization_barrier((mine, turned, index))
    pieces = near + [across(x) for x in near]
    here = (lax.axis_index("col") & 3).reshape(1)
    *sends, other = main(*index, here, blocks, *turned, pieces)
    parts = [sends[0]] + [along_y(sends[d], d) for d in range(1, 4)]
    other = sum_z(here, exchange_z(other))
    first = exchange_z(sum_y(parts))
    other = [other[0]] + [along_y(other[d], d) for d in range(1, 4)]
    return final(here, first, other).transpose(1, 0, 2)


def solution(mesh):
    return jax.shard_map(
        shards,
        mesh=mesh,
        in_specs=(
            jax.sharding.PartitionSpec(("row", "col"), None, None, None),
            jax.sharding.PartitionSpec(("row", "col"), None, None),
            jax.sharding.PartitionSpec(("row", "col"), None),
            jax.sharding.PartitionSpec(("row", "col")),
            jax.sharding.PartitionSpec(("row", "col"), None),
        ),
        out_specs=jax.sharding.PartitionSpec("row", None, "col"),
        check_vma=False,
    )
```

```python
import functools
import jax, jax.numpy as jnp
from jax import lax
from jax.experimental import pallas as pl
from jax.experimental.pallas import tpu as pltpu
bf, f32 = jnp.bfloat16, jnp.float32
B, K, KC, CR, R = 48, 27, 27, 16, 48
PAIRS = (K + 1) // 2
PIECE = R // 2 * B
HALF = B // 2
TILE = 8 * PIECE
FULL = (0, 2, 3, 5)
SPLIT = ((1, 0), (1, 1), (4, 0), (4, 1))

T = KC * CR
FIRST = 336
REST = T - FIRST
ROWS1 = FIRST * 72 // 128
PAD1 = 192
ROWS2 = REST * 72 // 128
PAD2 = 56

def pack_kernel(p_ref, o_ref):
    for g in range(R // 8):
        o_ref[g * B:(g + 1) * B, :] = jnp.concatenate([p_ref[8 * g + m] for m in range(8)], axis=1)

def pack(p):
    return pl.pallas_call(pack_kernel, out_shape=jax.ShapeDtypeStruct((R // 8 * B, 8 * B), bf))(p)

def placing(n, step, off):
    row = lax.broadcasted_iota(jnp.int32, (n * 128, 384), 0)
    col = lax.broadcasted_iota(jnp.int32, (n * 128, 384), 1)
    t, c = col // step, col % step
    return (row == (t // 2) * 128 + (t % 2) * B + off + c).astype(f32).astype(bf)

def turn_kernel(p_ref, o_ref, full_ref, half_ref):
    row = lax.broadcasted_iota(jnp.int32, (B, B), 0)
    a = lax.broadcasted_iota(jnp.int32, (B, B), 1)
    pick = (row == (a % 6) * 8 + a // 6).astype(f32).astype(bf)
    for i in range(R):
        o_ref[i] = lax.dot_general(pick, p_ref[i], (((1,), (1,)), ((), ())), preferred_element_type=f32).astype(bf)
    full_ref[...] = placing(4, B, 0)
    for h in range(2):
        half_ref[h] = placing(8, HALF, h * HALF)

def turn(p):
    return pl.pallas_call(turn_kernel, out_shape=[jax.ShapeDtypeStruct((R, B, B), bf), jax.ShapeDtypeStruct((512, 384), bf),
                                                  jax.ShapeDtypeStruct((2, 1024, 384), bf)],
                          cost_estimate=pl.CostEstimate(flops=10**7, bytes_accessed=2 * 10**6, transcendentals=0))(p)

def main_kernel(src, odd, dst, here, blk_hbm, turned_hbm, full_hbm, half_hbm, *rest):
    pieces, sends, out2, (stage, out, buf2, osems, blk, turned, tile, lo, hi, bufa, bufb, only, full_ref, half_ref, sems, psems) = (
        rest[:8], rest[8:12], rest[12], rest[13:])
    first = [pltpu.make_async_copy(piece, stage.at[pl.ds(n * (R // 8 * B), R // 8 * B)], psems.at[n]) for n, piece in enumerate(pieces)]
    first.append(pltpu.make_async_copy(turned_hbm, turned, psems.at[8]))
    CH = 4
    def copy(n):
        return pltpu.make_async_copy(blk_hbm.at[pl.ds(n * CH, CH)], blk.at[pl.ds(n * CH, CH)], sems.at[n])
    late = [pltpu.make_async_copy(full_hbm, full_ref, psems.at[9]), pltpu.make_async_copy(half_hbm, half_ref, psems.at[10])]
    for c in first:
        c.start()
    copy(0).start()

    def zero(n, c):
        z = pl.multiple_of(n * 384, 8)
        lo[pl.ds(z, 384), :] = jnp.zeros((384, 128), f32)
        hi[pl.ds(z, 384), :] = jnp.zeros((384, 128), f32)
        return c
    lax.fori_loop(0, T // 2 * B // 384, zero, 0)
    lane = lax.broadcasted_iota(jnp.int32, (32, 128), 1)
    row = lax.broadcasted_iota(jnp.int32, (32, 128), 0)
    only[...] = ((lane >= B * (row // 16)) & (lane < B * (row // 16) + B)).astype(f32).astype(bf)

    picks = []
    for p in range(4):
        start = 2 * B * p // 128 * 128
        wide = min(256, 8 * B - start)
        l0 = lax.broadcasted_iota(jnp.int32, (wide, 256), 0) + start - 2 * B * p
        l1 = lax.broadcasted_iota(jnp.int32, (wide, 256), 1)
        other = l1 - 128
        keep = (l1 < 2 * B) & (l0 == l1)
        change = (other >= 0) & (other < 2 * B) & (l0 == jnp.where(other < B, other + B, other - B))
        picks.append((start, wide, (keep | change).astype(f32).astype(bf)))
    side = R // 8 * B
    for q in range(2):
        for n in range(4 * q, 4 * q + 4):
            first[n].wait()
        if q == 1:
            for n in range(1, R // CH):
                copy(n).start()
            for c in late:
                c.start()
        for p, (start, wide, pick) in enumerate(picks):
            x = stage[4 * q * side:4 * (q + 1) * side, start:start + wide]
            x = jnp.dot(x, pick, preferred_element_type=f32).astype(bf)
            at = (2 * p + q) * 4 * side
            tile[at:at + 4 * side, :] = x[:, :128]
            tile[TILE + at:TILE + at + 4 * side, :] = x[:, 128:]
    first[8].wait()

    def phase1(i, n, buf):
        ks = list(range(2 * n, min(2 * n + 2, K)))
        w = []
        for k in ks:
            mask = only[pl.ds(pl.multiple_of(odd[k, i], 16), 16), :]
            w.append(tile[pl.ds(pl.multiple_of(src[k, i], B), B), :] * jnp.concatenate([mask] * 3, axis=0))
        if len(ks) == 2:
            none = jnp.zeros((B, 128), bf)
            lhs = jnp.concatenate([blk[i, ks[0]], blk[i, ks[1]]], axis=1)
            w = jnp.concatenate([jnp.concatenate([w[0], none], axis=1), jnp.concatenate([none, w[1]], axis=1)], axis=0)
            buf[:, n * 256:(n + 1) * 256] = jnp.dot(lhs, w, preferred_element_type=f32).astype(bf)
        else:
            buf[:, n * 256:n * 256 + 128] = jnp.dot(blk[i, ks[0]], w[0], preferred_element_type=f32).astype(bf)

    def phase2(i, n, buf):
        wide = min(4, K - 2 * n) * 128
        term = jnp.dot(turned[i], buf[:, n * 256:n * 256 + wide], preferred_element_type=f32)
        for m in range(wide // 128):
            k = 2 * n + m
            acc = hi if m & 1 else lo
            acc[pl.ds(pl.multiple_of(dst[k, i], B), B), :] += term[:, m * 128:(m + 1) * 128]

    def both(i1, buf1, i2, buf2):
        for n in range(0, PAIRS, 2):
            phase2(i2, n, buf2)
            phase1(i1, n, buf1)
            phase1(i1, n + 1, buf1)

    copy(0).wait()
    for n in range(PAIRS):
        phase1(0, n, bufa)
    def rows(p, c):
        both(2 * p + 1, bufb, 2 * p, bufa)
        @pl.when((p & 1 == 1) & (p < R // 2 - 1))
        def _():
            copy((p + 1) // 2).wait()
        both(jnp.minimum(2 * p + 2, R - 1), bufa, 2 * p + 1, bufb)
        return c
    lax.fori_loop(0, R // 2, rows, 0)

    def gathered(t2, u, each, groups):
        cols_ = []
        for n in range(each):
            rows_ = []
            for g in range(groups):
                at = (t2 + g * each + n) * B + 8 * u
                rows_.append(lo[at:at + 8, :] + hi[at:at + 8, :])
            cols_.append(jnp.concatenate(rows_, axis=0).astype(bf))
        return cols_
    def pack_rows(t, y, half, xs, place):
        step = B if half else 2 * B
        for w in range(3):
            n0, n1 = 128 * w // step, (128 * w + 127) // step + 1
            x = jnp.dot(jnp.concatenate(xs[n0:n1], axis=1), place[n0 * 128:n1 * 128, w * 128:w * 128 + 128], preferred_element_type=f32)
            for g in range(x.shape[0] // 8):
                v = x[8 * g:8 * g + 8, :]
                if t < FIRST:
                    at = (FIRST * B // 128 + t * HALF // 128 if half else t * B // 128) + g * 3 + w
                    out[y, :, at * 128:at * 128 + 128] = v.astype(bf)
                else:
                    buf2[pl.ds(y * PAD2 + (REST * B // 128 if half else 0) + g * 3 + w, 8, stride=4 * PAD2), :] = v
    away = [pltpu.make_async_copy(out.at[(here[0] + d) & 3], sends[d], osems.at[d]) for d in range(4)]
    for c in late:
        c.wait()
    for t, count in ((0, FIRST), (FIRST, REST)):
        for y, u in enumerate(FULL):
            pack_rows(t, y, False, gathered(t // 2, u, 4, count // 8), full_ref)
        for u in (1, 4):
            xs = gathered(t // 2, u, 8, count // 16)
            for y, (v, h) in enumerate(SPLIT):
                if v == u:
                    pack_rows(t, y, True, xs, half_ref.at[h])
        if t == 0:
            for c in away:
                c.start()
    for z in range(8):
        out2[z] = buf2[z * 4 * PAD2:(z + 1) * 4 * PAD2, :].astype(bf)
    for c in away:
        c.wait()

def main(src, odd, dst, here, blocks, turned, full, half, pieces):
    hbm = pl.BlockSpec(memory_space=pl.ANY)
    vmem = pl.BlockSpec(memory_space=pltpu.VMEM)
    return pl.pallas_call(
        main_kernel,
        out_shape=[jax.ShapeDtypeStruct((8, FIRST * 72), bf)] * 4 + [jax.ShapeDtypeStruct((8, 4 * PAD2, 128), bf)],
        in_specs=[pl.BlockSpec(memory_space=pltpu.SMEM)] * 4 + [hbm] * 12,
        out_specs=[hbm] * 4 + [vmem],
        scratch_shapes=[pltpu.VMEM((8 * (R // 8 * B), 8 * B), bf), pltpu.VMEM((4, 8, FIRST * 72), bf), pltpu.VMEM((8 * 4 * PAD2, 128), f32), pltpu.SemaphoreType.DMA((4,)),
                        pltpu.VMEM((R, K, B, B), bf), pltpu.VMEM((R, B, B), bf), pltpu.VMEM((2 * TILE, 128), bf)]
            + [pltpu.VMEM((T // 2 * B, 128), f32)] * 2 + [pltpu.VMEM((B, PAIRS * 256), bf)] * 2
            + [pltpu.VMEM((32, 128), bf), pltpu.VMEM((512, 384), bf), pltpu.VMEM((2, 1024, 384), bf)]
            + [pltpu.SemaphoreType.DMA((12,)), pltpu.SemaphoreType.DMA((11,))],
        compiler_params=pltpu.CompilerParams(vmem_limit_bytes=58 << 20),
        cost_estimate=pl.CostEstimate(flops=2 * 10**10, bytes_accessed=10**7, transcendentals=0),
    )(src, odd, dst, here, blocks, turned, full, half, *pieces)

def sum_y_kernel(x0, x1, x2, x3, o_ref, buf):
    def body(b, c):
        at = pl.multiple_of(b * 128, 128)
        s = (x0[:, pl.ds(at, 128)].astype(f32) + x1[:, pl.ds(at, 128)].astype(f32)) + (
            x2[:, pl.ds(at, 128)].astype(f32) + x3[:, pl.ds(at, 128)].astype(f32))
        buf[pl.ds(b, 8, stride=PAD1), :] = s
        return c
    lax.fori_loop(0, ROWS1, body, 0, unroll=21)
    for z in range(8):
        o_ref[z] = buf[z * PAD1:(z + 1) * PAD1, :].astype(bf)

def sum_y(parts):
    return pl.pallas_call(sum_y_kernel, out_shape=jax.ShapeDtypeStruct((8, PAD1, 128), bf),
                          scratch_shapes=[pltpu.VMEM((8 * PAD1, 128), f32)],
                          cost_estimate=pl.CostEstimate(flops=4 * 10**10, bytes_accessed=10**7, transcendentals=0))(*parts)

def sum_z_kernel(here, x_ref, *refs):
    outs, tot = refs[:4], refs[4]
    tot[...] = functools.reduce(lambda p, q: p + q, [x_ref[z].astype(f32) for z in range(8)])
    for d in range(4):
        outs[d][...] = tot[pl.ds(pl.multiple_of(((here[0] + d) & 3) * PAD2, 8), PAD2), :].astype(bf)

def sum_z(here, x):
    return pl.pallas_call(sum_z_kernel, out_shape=[jax.ShapeDtypeStruct((PAD2, 128), bf)] * 4,
                          in_specs=[pl.BlockSpec(memory_space=pltpu.SMEM), pl.BlockSpec(memory_space=pltpu.VMEM)],
                          scratch_shapes=[pltpu.VMEM((4 * PAD2, 128), f32)])(here, x)

def final_kernel(here, x_ref, y0, y1, y2, y3, o_ref, tot1, tot2):
    tot1[...] = functools.reduce(lambda p, q: p + q, [x_ref[z].astype(f32) for z in range(8)])
    tot2[...] = functools.reduce(lambda p, q: p + q, [y[...].astype(f32) for y in (y0, y1, y2, y3)])
    odd = here[0] & 1
    l0 = lax.broadcasted_iota(jnp.int32, (384, 128), 0)
    l1 = lax.broadcasted_iota(jnp.int32, (384, 128), 1)
    for tot, total, slot in ((tot1, FIRST, 0), (tot2, REST, FIRST // CR)):
        acc = jnp.zeros((total, 128), f32)
        for step, start, place in ((B, 0, odd * HALF), (HALF, total * B // 128, (1 - odd) * B)):
            side = 384 // step
            groups = total // side
            pick = (l0 % step + place == l1).astype(f32).astype(bf)
            lane = lax.broadcasted_iota(jnp.int32, (1, side, 128), 2)
            which = lax.broadcasted_iota(jnp.int32, (1, side, 128), 1)
            xs = [tot[pl.ds(start + w, groups, stride=3), :] for w in range(3)]
            for _ in range(3):
                wide = []
                for w in range(3):
                    top = xs[w].astype(bf).astype(f32)
                    xs[w] = xs[w] - top
                    mine = (lane + w * 128) // step == which
                    wide.append(jnp.where(mine, top[:, None, :], 0.0).reshape(total, 128).astype(bf))
                acc = acc + jnp.dot(jnp.concatenate(wide, axis=1), pick, preferred_element_type=f32)
        o_ref[slot:slot + total // CR] = acc[:, :72].reshape(total // CR, CR, 72)

def final(here, x, parts):
    return pl.pallas_call(final_kernel, out_shape=jax.ShapeDtypeStruct((KC, CR, 72), f32),
                          in_specs=[pl.BlockSpec(memory_space=pltpu.SMEM)] + [pl.BlockSpec(memory_space=pltpu.VMEM)] * 5,
                          scratch_shapes=[pltpu.VMEM((PAD1, 128), f32), pltpu.VMEM((PAD2, 128), f32)])(here, x, *parts)

ZG = [[z * 4 + y for z in range(8)] for y in range(4)]

def along_x(x, by):
    return lax.ppermute(x, "row", [(i, (i + 2 * by) % 8) for i in range(8)])

def across(x):
    return lax.ppermute(x, "row", [(i, i ^ 1) for i in range(8)])

def along_y(x, by):
    return lax.ppermute(x, "col", [(4 * z + y, 4 * z + (y + by) % 4) for z in range(8) for y in range(4)])

def exchange_z(x):
    return lax.all_to_all(x, "col", 0, 0, axis_index_groups=ZG, tiled=True)

def indices(columns, aggregate, slots):
    row = lax.axis_index("row")
    owner = columns // R
    apart = ((owner >> 1) - (row >> 1)) & 3
    piece = jnp.where(apart == 3, 2, jnp.where(apart == 2, 3, apart)) + 4 * ((owner ^ row) & 1)
    t = columns % R
    at = ((t & 7) >> 1) * R + piece * (R // 8) + (t >> 3)
    target = slots * CR + aggregate[:, None]
    odd = target & 1
    return (at * B + ((t ^ odd) & 1) * TILE).T, (odd * 16).T, ((target >> 1) * B).T

def shards(blocks, prolong, columns, aggregate, slots):
    packed = pack(prolong)
    mine = [packed, along_x(packed, -1), along_x(packed, 1), along_x(packed, 2)]
    index = indices(columns, aggregate, slots)
    turned = turn(prolong)
    near, turned, index = lax.optimization_barrier((mine, turned, index))
    pieces = near + [across(x) for x in near]
    here = (lax.axis_index("col") & 3).reshape(1)
    *sends, other = main(*index, here, blocks, *turned, pieces)
    parts = [sends[0]] + [along_y(sends[d], d) for d in range(1, 4)]
    other = sum_z(here, exchange_z(other))
    first = exchange_z(sum_y(parts))
    other = [other[0]] + [along_y(other[d], d) for d in range(1, 4)]
    return final(here, first, other).transpose(1, 0, 2)


def solution(mesh):
    return jax.shard_map(
        shards,
        mesh=mesh,
        in_specs=(
            jax.sharding.PartitionSpec(("row", "col"), None, None, None),
            jax.sharding.PartitionSpec(("row", "col"), None, None),
            jax.sharding.PartitionSpec(("row", "col"), None),
            jax.sharding.PartitionSpec(("row", "col")),
            jax.sharding.PartitionSpec(("row", "col"), None),
        ),
        out_specs=jax.sharding.PartitionSpec("row", None, "col"),
        check_vma=False,
    )
```
